256 devices in a mesh: wide: 32 (over x, y, core), narrow: 8 (over z).
Axes of the slice: x: 4, y: 4, z: 8, core: 2. Of those that a mesh axis runs over, the one named last changes fastest.
Arguments:
- sources: float32 [32, 8, 16, 2, 512], P('wide', 'narrow'), may hold values from -6 to 6
- schur_blocks: bfloat16 [32, 8, 2048, 2048], P('wide', 'narrow'), as said below
- scaling: float32 [32, 8, 2, 512], P('wide', 'narrow'), may hold values from 0.08 to 0.4
- coarse_basis: float32 [32, 8, 2, 2, 8, 512], P('wide', 'narrow'), may hold values from -0.09375 to 0.09375
- coarse_inverse: float32 [32, 80, 80], P('wide'), as said below
- face_sizes: int32 [32, 8, 2], P('wide', 'narrow'), may hold values from 0 to 512, as said below
- face_match: int32 [32, 8, 2, 512], P('wide', 'narrow'), may hold values from 0 to 511, as said below
- face_slots: int32 [32, 8, 4], P('wide', 'narrow'), may hold values from 0 to 3, each once within a row
- corner_slots: int32 [33, 9], replicated, may hold values from 0 to 319, as said below
Outputs:
- solution: float32 [32, 8, 16, 2, 512], P('wide', 'narrow')
- residual: float32 [32, 8, 16, 2, 512], P('wide', 'narrow')
The draws below stay inside these ranges and needn't reach their ends.
Inputs may be any that keep to these rules, and one draw needn't show every extreme that they name: `face_sizes`: the east faces of the last wide index and the north faces of the last narrow index have 0 unknowns; every other face has 128 to 512, and some face has exactly 512. `face_match`: each block is a permutation of 0 to 511 that maps the positions below the size of the matching owned face onto themselves. `corner_slots`: distinct slots for distinct vertices; slot 319 is used. `schur_blocks`: each block is symmetric and positive definite. `coarse_inverse`: each block is symmetric and positive definite.
All inputs are finite; a program needn't handle non-finite values.
Results may differ from the reference program's by a relative error of at most 0.0052.
Values may be sent and summed in bfloat16 or wider, within the bound.
A program may use at most 64 MiB of HBM per device.

```python
import math
import jax
import jax.numpy as jnp
from jax import lax

FACE = 512
NRHS = 16
NCD = 8
ITERS = 2
NI = 2048
SUBW = 32
SUBN = 8
VERTS = 297
SLOTS = 320
CB = 80


def spd_blocks(key, count, order, diagonal):

    def single(position):
        subkey = jax.random.fold_in(key, position)
        entries = jax.random.normal(subkey, (order, order), jnp.float32)
        symmetric = (entries + entries.T) * (0.70710678 / order ** 0.5)
        matrix = symmetric + diagonal * jnp.eye(order, dtype=jnp.float32)
        return matrix
    return lax.map(single, jnp.arange(count, dtype=jnp.int32))


def draw_schur_blocks(key, part):
    blocks = spd_blocks(jax.random.fold_in(key, 3), SUBW * SUBN, NI, 3.0)
    return blocks.astype(jnp.bfloat16).reshape(SUBW, SUBN, NI, NI)


def draw_coarse_inverse(key, part):
    return spd_blocks(jax.random.fold_in(key, 5), SUBW, CB, 5.0)


def face_lengths(key):
    random_len = jax.random.randint(jax.random.fold_in(key, 11), (SUBW, SUBN, 2), FACE // 4, FACE + 1)
    wide_pos = lax.broadcasted_iota(jnp.int32, (SUBW, SUBN, 2), 0)
    narrow_pos = lax.broadcasted_iota(jnp.int32, (SUBW, SUBN, 2), 1)
    face_kind = lax.broadcasted_iota(jnp.int32, (SUBW, SUBN, 2), 2)
    interior = jnp.where(face_kind == 0, wide_pos < SUBW - 1, narrow_pos < SUBN - 1)
    chosen_wide = jax.random.randint(jax.random.fold_in(key, 12), (), 0, SUBW - 1)
    chosen_narrow = jax.random.randint(jax.random.fold_in(key, 13), (), 0, SUBN)
    is_full = (wide_pos == chosen_wide) & (narrow_pos == chosen_narrow) & (face_kind == 0)
    return jnp.where(interior, jnp.where(is_full, FACE, random_len), 0).astype(jnp.int32)


def draw_face_sizes(key, part):
    return face_lengths(key)


def draw_face_match(key, part):
    lengths = face_lengths(key)
    west_len = jnp.concatenate([jnp.zeros((1, SUBN), jnp.int32), lengths[:-1, :, 0]], axis=0)
    south_len = jnp.concatenate([jnp.zeros((SUBW, 1), jnp.int32), lengths[:, :-1, 1]], axis=1)
    incoming = jnp.stack([west_len, south_len], axis=-1)
    subkeys = jax.random.split(jax.random.fold_in(key, 21), SUBW * SUBN * 2)
    orders = jax.vmap(lambda subkey: jax.random.permutation(subkey, FACE))(subkeys).reshape(SUBW, SUBN, 2, FACE)
    position = lax.broadcasted_iota(jnp.int32, (SUBW, SUBN, 2, FACE), 3)
    scores = orders.astype(jnp.int32) + FACE * (position >= incoming[:, :, :, None]).astype(jnp.int32)
    return jnp.argsort(scores, axis=-1).astype(jnp.int32)


def draw_corner_slots(key, part):
    leading = jax.random.permutation(jax.random.fold_in(key, 31), SLOTS - 1)[:VERTS - 1].astype(jnp.int32)
    chosen = jnp.concatenate([leading, jnp.full((1,), SLOTS - 1, jnp.int32)])
    shuffled = jax.random.permutation(jax.random.fold_in(key, 32), chosen)
    return shuffled.reshape(SUBW + 1, SUBN + 1).astype(jnp.int32)


def shard_levels(key, extent, cuts, low, top_value):
    def one(dim, shards_of):
        heights = jax.random.uniform(jax.random.fold_in(jax.random.fold_in(key, 6), dim), (shards_of,), jnp.float32, low / len(cuts), top_value / len(cuts))
        return jnp.repeat(jnp.exp(heights), extent[dim] // shards_of).reshape((-1,) + (1,) * (len(extent) - dim - 1))

    gain = one(*cuts[0])
    for cut in cuts[1:]:
        gain = gain * one(*cut)
    return gain


def bell_draw(key, extent, spread, reach, shards=(), held_as=jnp.bfloat16):
    values = spread * jax.random.normal(key, extent, jnp.float32)
    if shards:
        values = values * shard_levels(key, extent, shards, -0.22, 0.18)
    return jnp.clip(values, -reach, reach).astype(held_as)


def setup_inputs(seed: int = 0) -> dict:
    arg_keys = jax.random.split(jax.random.key(seed), 10)
    sources = bell_draw(arg_keys[0], (SUBW, SUBN, NRHS, 2, FACE), 1.0, 6.0, ((0, 32), (1, 8)), jnp.float32)
    schur_blocks = draw_schur_blocks(jax.random.fold_in(arg_keys[9], 71), 0)
    scaling = jnp.clip(jnp.exp(math.log(0.4) - 1.609438 * jax.random.uniform(arg_keys[2], (SUBW, SUBN, 2, FACE), jnp.float32) ** shard_levels(arg_keys[2], (SUBW, SUBN, 2, FACE), ((0, 32), (1, 8)), -0.2, 0.2)), 0.08, 0.4)
    coarse_basis = bell_draw(arg_keys[3], (SUBW, SUBN, 2, 2, NCD, FACE), (FACE * NCD) ** -0.5, 0.09375, ((0, 32), (1, 8)), jnp.float32)
    coarse_inverse = draw_coarse_inverse(jax.random.fold_in(arg_keys[9], 71), 0)
    face_sizes = draw_face_sizes(jax.random.fold_in(arg_keys[9], 71), 0)
    face_match = draw_face_match(jax.random.fold_in(arg_keys[9], 71), 0)
    face_slots = jax.vmap(lambda own: jax.random.permutation(own, 4))(jax.random.split(arg_keys[7], SUBW * SUBN)).reshape((SUBW, SUBN, 4)).astype(jnp.int32)
    corner_slots = draw_corner_slots(jax.random.fold_in(arg_keys[9], 71), 0)
    return dict(sources=sources, schur_blocks=schur_blocks, scaling=scaling, coarse_basis=coarse_basis, coarse_inverse=coarse_inverse, face_sizes=face_sizes, face_match=face_match, face_slots=face_slots, corner_slots=corner_slots)


highest = lax.Precision.HIGHEST


def reference(sources, schur_blocks, scaling, coarse_basis, coarse_inverse, face_sizes, face_match, face_slots, corner_slots):
    subw = sources.shape[0]
    subn = sources.shape[1]
    nrhs_count = sources.shape[2]
    face_width = sources.shape[4]
    basis_count = coarse_basis.shape[4]
    block_order = coarse_inverse.shape[1]
    slot_count = block_order // basis_count * subw
    places = jnp.arange(face_width, dtype=jnp.int32)
    live_mask = (places[None, None, None, :] < face_sizes[:, :, :, None]).astype(jnp.float32)
    weights = scaling * live_mask
    vectors = coarse_basis * live_mask[:, :, :, None, None, :]
    backward = jnp.argsort(face_match, axis=-1).astype(jnp.int32)
    slot_table = (face_slots[:, :, :, None] == jnp.arange(4, dtype=jnp.int32)[None, None, None, :]).astype(jnp.float32)
    corner_ids = jnp.stack([corner_slots[1:, :-1], corner_slots[1:, 1:], corner_slots[:-1, 1:], corner_slots[1:, 1:]], axis=-1)
    initial = sources * live_mask[:, :, None]

    def multiply(pair):
        vector, block_matrix = pair
        return jnp.dot(vector, block_matrix, preferred_element_type=jnp.float32)

    def apply_operator(direction):
        rounded = direction.astype(jnp.bfloat16)
        east_faces = rounded[:, :, :, 0]
        north_faces = rounded[:, :, :, 1]
        from_west = jnp.concatenate([jnp.zeros_like(east_faces[:1]), east_faces[:-1]], axis=0)
        from_south = jnp.concatenate([jnp.zeros_like(north_faces[:, :1]), north_faces[:, :-1]], axis=1)
        west_face = jnp.take_along_axis(from_west, jnp.broadcast_to(face_match[:, :, None, 0, :], from_west.shape), axis=3)
        south_face = jnp.take_along_axis(from_south, jnp.broadcast_to(face_match[:, :, None, 1, :], from_south.shape), axis=3)
        stacked = jnp.stack([east_faces, north_faces, west_face, south_face], axis=3).astype(jnp.float32)
        slotted = jnp.einsum("wnrdk,wnds->wnrsk", stacked, slot_table, precision=highest).astype(jnp.bfloat16)
        product = lax.map(multiply, (slotted.reshape(subw * subn, nrhs_count, 4 * face_width), schur_blocks.reshape(subw * subn, 4 * face_width, 4 * face_width)))
        by_face = jnp.einsum("wnrsk,wnds->wnrdk", product.reshape(subw, subn, nrhs_count, 4, face_width), slot_table, precision=highest)
        to_west = jnp.take_along_axis(by_face[:, :, :, 2], jnp.broadcast_to(backward[:, :, None, 0, :], from_west.shape), axis=3)
        to_south = jnp.take_along_axis(by_face[:, :, :, 3], jnp.broadcast_to(backward[:, :, None, 1, :], from_south.shape), axis=3)
        from_east = jnp.concatenate([to_west[1:], jnp.zeros_like(to_west[:1])], axis=0)
        from_north = jnp.concatenate([to_south[:, 1:], jnp.zeros_like(to_south[:, :1])], axis=1)
        summed_all = jnp.stack([by_face[:, :, :, 0] + from_east, by_face[:, :, :, 1] + from_north], axis=3)
        return summed_all * live_mask[:, :, None]

    def precondition(residual):
        partial_value = jnp.einsum("wnfemk,wnrfk->wnfemr", vectors, residual, precision=highest).reshape(subw, subn, 4, basis_count, nrhs_count)
        gathered = jnp.zeros((slot_count, basis_count, nrhs_count), jnp.float32).at[corner_ids].add(partial_value)
        grouped = gathered.reshape(subw, block_order, nrhs_count)
        solved = jnp.einsum("bij,bjr->bir", coarse_inverse, grouped, precision=highest).reshape(slot_count, basis_count, nrhs_count)
        local_values = solved[corner_ids].reshape(subw, subn, 2, 2, basis_count, nrhs_count)
        return weights[:, :, None] * residual + jnp.einsum("wnfemk,wnfemr->wnrfk", vectors, local_values, precision=highest)

    def inner(left, right):
        return jnp.sum(left * right, axis=(0, 1, 3, 4))

    residual = initial
    solution = jnp.zeros_like(initial)
    precond = precondition(residual)
    direction = precond
    inner_now = inner(residual, precond)
    for iteration in range(ITERS):
        applied = apply_operator(direction)
        step_size = inner_now / inner(direction, applied)
        solution = solution + step_size[None, None, :, None, None] * direction
        residual = residual - step_size[None, None, :, None, None] * applied
        if iteration + 1 < ITERS:
            precond = precondition(residual)
            inner_new = inner(residual, precond)
            direction = precond + (inner_new / inner_now)[None, None, :, None, None] * direction
            inner_now = inner_new
    return solution, residual
```

```python
import jax
import jax.numpy as jnp
from jax import lax
from jax.experimental import pallas as pl
from jax.experimental.pallas import tpu as pltpu
from jax.sharding import PartitionSpec as P

MESH = pl.DeviceIdType.MESH
f32 = jnp.float32
bf16 = jnp.bfloat16
NT = (((1,), (1,)), ((), ()))
EAST, NORTH, WEST, SOUTH = range(4)


def iota(shape, dim):
    return lax.broadcasted_iota(jnp.int32, shape, dim)


def mm(a, b):
    return jnp.dot(a, b, preferred_element_type=f32)


def mm_nt(a, b):
    return lax.dot_general(a, b, NT, preferred_element_type=f32)


def split(x):
    high = x.astype(bf16)
    return high, (x - high.astype(f32)).astype(bf16)


def halves(x):
    return jnp.concatenate(split(x), axis=0)


def fold(x):
    rows = x.shape[0] // 2
    return x[:rows] + x[rows:]


def kernel(
    sizes,
    slots,
    corners,
    src,
    schur,
    scaling,
    basis,
    inverse,
    match,
    row_slots,
    sol_out,
    res_out,
    blocks,
    faces,
    lift,
    perm,
    pick,
    coef,
    inverses,
    zmsg,
    zbuf,
    wmsg,
    wbuf,
    zlast,
    zlast_buf,
    wlast,
    wlast_buf,
    fore_out,
    fore_in,
    flux_out,
    flux_in,
    back_out,
    back_in,
    load_sem,
    z_send,
    z_recv,
    w_send,
    w_recv,
    fore_send,
    fore_recv,
    flux_send,
    flux_recv,
    back_send,
    back_recv,
    inv_send,
    inv_recv,
):
    wide_count = lax.axis_size("wide")
    narrow_count = lax.axis_size("narrow")
    wide_at = lax.axis_index("wide")
    narrow_at = lax.axis_index("narrow")
    count = src.shape[0]
    width = src.shape[2]
    order = inverse.shape[0]
    modes = basis.shape[2]
    capacity = order // modes
    lanes = modes * count
    corner_rows = 4 * modes
    msg_rows = wmsg.shape[1]

    def z_peer(k):
        return (wide_at, lax.rem(narrow_at + 1 + k, narrow_count))

    def w_peer(k):
        return (lax.rem(wide_at + 1 + k, wide_count), narrow_at)

    east = (lax.rem(wide_at + 1, wide_count), narrow_at)
    west = (lax.rem(wide_at + wide_count - 1, wide_count), narrow_at)
    north = (wide_at, lax.rem(narrow_at + 1, narrow_count))
    south = (wide_at, lax.rem(narrow_at + narrow_count - 1, narrow_count))

    barrier = pltpu.get_barrier_semaphore()

    def greet(peer, number):
        def one(k, carry):
            pl.semaphore_signal(barrier, 1, device_id=peer(k), device_id_type=MESH)
            return carry

        lax.fori_loop(0, number, one, 0)

    greet(z_peer, narrow_count - 1)
    greet(w_peer, wide_count - 1)

    for s in range(4):
        for t in range(4):
            pltpu.make_async_copy(
                schur.at[pl.ds(s * width, width), pl.ds(t * width, width)],
                blocks.at[s, t],
                load_sem,
            ).start()

    def remote(a, b, send, recv, device):
        return pltpu.make_async_remote_copy(
            src_ref=a, dst_ref=b, send_sem=send, recv_sem=recv, device_id=device, device_id_type=MESH
        )

    def spread(a, b, send, recv, peer, number):
        def one(k, carry):
            remote(a, b, send, recv, peer(k)).start()
            return carry

        lax.fori_loop(0, number, one, 0)

    def drain(ref, number, sem):
        part = ref.at[pl.ds(0, number)]
        pltpu.make_async_copy(part, part, sem).wait()

    place = iota((1, width), 1)
    live = [(place < sizes[0, f]).astype(f32) for f in range(2)]
    weight = [scaling[f : f + 1, :] * live[f] for f in range(2)]
    residual = [src[:, f, :] * live[f] for f in range(2)]
    scaled = [residual[f] * weight[f] for f in range(2)]
    vec = [[basis[f, e] * live[f] for e in range(2)] for f in range(2)]
    nothing = jnp.zeros((modes, width), f32)

    for f in range(2):
        fore_out[f, 0 : 2 * count, :] = halves(scaled[f])
        fore_out[f, 2 * count : 4 * count, :] = halves(jnp.concatenate(vec[f], axis=0))

    def set_face(d, scaled_parts, ends):
        faces[d, 0 : 2 * count, :] = scaled_parts
        faces[d, 2 * count : 2 * count + 2 * corner_rows, :] = ends

    set_face(
        EAST,
        halves(scaled[0]),
        halves(jnp.concatenate([nothing, nothing, vec[0][0], vec[0][1]], axis=0)),
    )
    set_face(
        NORTH,
        halves(scaled[1]),
        halves(jnp.concatenate([nothing, vec[1][0], nothing, vec[1][1]], axis=0)),
    )

    wide_lanes = 4 * lanes
    grow = ((iota((2 * corner_rows, wide_lanes), 0) & (corner_rows - 1)) == iota((2 * corner_rows, wide_lanes), 1) // count).astype(bf16)
    own_lane = iota((count, wide_lanes), 1) % count == iota((count, wide_lanes), 0)
    own_lane_one = own_lane[:, 0:lanes]

    def restrict(pairs):
        total = 0.0
        for values, d in pairs:
            total = total + mm_nt(
                halves(values), faces[d, 2 * count : 2 * count + 2 * corner_rows, :]
            )
        spread_out = fold(mm(halves(fold(total)), grow))
        row = jnp.sum(jnp.where(own_lane, spread_out, 0.0), axis=0, keepdims=True)
        return jnp.concatenate([row[:, v * lanes : (v + 1) * lanes] for v in range(4)], axis=0)

    def inner(pairs):
        total = 0.0
        for a, b in pairs:
            total = total + jnp.sum(a * b, axis=1, keepdims=True)
        return total

    lane_one = iota((count, lanes), 1)
    row_one = iota((count, lanes), 0)

    def pack(values):
        out = jnp.zeros((count, lanes), f32)
        for g, value in enumerate(values):
            out = out + jnp.where(lane_one == g * count + row_one, value, 0.0)
        return jnp.sum(out, axis=0, keepdims=True)

    def unpack(row, g):
        return jnp.sum(jnp.where(lane_one == g * count + row_one, row, 0.0), axis=1, keepdims=True)

    def as_row(value):
        return jnp.sum(jnp.where(own_lane_one, value, 0.0), axis=0, keepdims=True)

    first = restrict([(residual[0], EAST), (residual[1], NORTH)])
    zmsg[0] = jnp.concatenate([first, jnp.zeros((4, lanes), f32)], axis=0)

    pl.semaphore_wait(barrier, narrow_count - 1 + wide_count - 1)

    def z_start(g):
        spread(zmsg.at[g], zbuf.at[g, narrow_at], z_send.at[g], z_recv.at[g], z_peer, narrow_count - 1)
        zbuf[g, narrow_at] = zmsg[g]

    msg_at = iota((msg_rows, 8 * narrow_count), 0)
    from_at = iota((msg_rows, 8 * narrow_count), 1)
    from_row = from_at & 7
    from_sub = from_at // 8
    verts = narrow_count + 1
    merge = (
        ((from_row == 0) & (msg_at == from_sub))
        | ((from_row == 1) & (msg_at == from_sub + 1))
        | ((from_row == 2) & (msg_at == from_sub + verts))
        | ((from_row == 3) & (msg_at == from_sub + verts + 1))
        | ((from_row == 4) & (msg_at == 2 * verts))
    ).astype(bf16)

    def w_start(g):
        drain(zbuf.at[g], narrow_count - 1, z_recv.at[g])
        high, low = split(zbuf[g].reshape(8 * narrow_count, lanes))
        wmsg[g] = mm(merge, high) + mm(merge, low)
        spread(wmsg.at[g], wbuf.at[g, wide_at], w_send.at[g], w_recv.at[g], w_peer, wide_count - 1)
        wbuf[g, wide_at] = wmsg[g]

    z_start(0)
    fore = [
        remote(fore_out.at[f], fore_in.at[f], fore_send.at[f], fore_recv.at[f], (east, north)[f])
        for f in range(2)
    ]
    for copy in fore:
        copy.start()
    spread(inverse, inverses.at[wide_at], inv_send, inv_recv, w_peer, wide_count - 1)
    inverses[wide_at] = inverse[...]

    for f in range(2):
        perm[f] = (iota((width, width), 0) == match[f : f + 1, :]).astype(bf16)
    low_wide = lax.axis_index("wide")
    vertex = [
        corners[low_wide, narrow_at],
        corners[low_wide, narrow_at + 1],
        corners[low_wide + 1, narrow_at],
        corners[low_wide + 1, narrow_at + 1],
    ]
    owner = [lax.div(v, capacity) for v in vertex]
    place_in = [v - b * capacity for v, b in zip(vertex, owner)]
    total_rows = wide_count * msg_rows
    for v in range(4):
        wanted = owner[v] * capacity + iota((order, total_rows), 0) // modes
        pick[v * order : (v + 1) * order, :] = (wanted == row_slots[...]).astype(f32).astype(bf16)
    pick[4 * order : 4 * order + 16, :] = (iota((16, total_rows), 1) % msg_rows == 2 * verts).astype(f32).astype(bf16)

    w_start(0)

    for f, copy in enumerate(fore):
        copy.wait_recv()
        got = mm(fore_in[f], perm[f])
        parts = []
        for base in (2 * count, 2 * count + 2 * modes):
            low_end = got[base : base + modes]
            high_end = got[base + modes : base + 2 * modes]
            if f == 0:
                parts += [low_end, high_end, nothing, nothing]
            else:
                parts += [low_end, nothing, high_end, nothing]
        set_face(
            WEST + f,
            got[0 : 2 * count].astype(bf16),
            jnp.concatenate(parts, axis=0).astype(bf16),
        )
    pltpu.make_async_copy(blocks, blocks, load_sem).wait()

    slot = [slots[0, d] for d in range(4)]
    base_out = []
    base_in = []
    for d in range(4):
        out = 0.0
        for s in range(4):
            out = out + mm(faces[s], blocks[slot[s], slot[d]])
        base_out.append(out[0:count] + out[count : 2 * count])
        high, low = split(
            out[2 * count : 2 * count + corner_rows]
            + out[2 * count + corner_rows : 2 * count + 2 * corner_rows]
        )
        lift[d, 0:corner_rows] = high
        lift[d, corner_rows : 2 * corner_rows] = high
        lift[d, 2 * corner_rows : 3 * corner_rows] = low
        lift[d, 3 * corner_rows :] = jnp.zeros((corner_rows, width), bf16)
        high = faces[d, 2 * count : 2 * count + corner_rows]
        lift[4 + d, 0:corner_rows] = high
        lift[4 + d, corner_rows : 2 * corner_rows] = high
        lift[4 + d, 2 * corner_rows : 3 * corner_rows] = faces[
            d, 2 * count + corner_rows : 2 * count + 2 * corner_rows
        ]
        lift[4 + d, 3 * corner_rows :] = jnp.zeros((corner_rows, width), bf16)
        base_in.append(
            faces[d, 0:count].astype(f32) + faces[d, count : 2 * count].astype(f32)
        )

    drain(inverses, wide_count - 1, inv_recv)
    for v in range(4):
        take = (iota((order, lanes), 0) == place_in[v] * modes + iota((order, lanes), 1) // count).astype(f32).astype(bf16)
        coef[v * order : (v + 1) * order, :] = fold(mm(halves(inverses[owner[v]]), take))

    tile = ((iota((2 * lanes, lanes), 0) % count) == (iota((2 * lanes, lanes), 1) % count)).astype(bf16)
    mode_lane = iota((4 * order, lanes), 1) // count == (iota((4 * order, lanes), 0) & (modes - 1))

    def gathered(g):
        drain(wbuf.at[g], wide_count - 1, w_recv.at[g])
        parts = jnp.concatenate(split(wbuf[g].reshape(total_rows, lanes)), axis=1)
        picked = mm(pick[...], parts)
        picked = picked[:, 0:lanes] + picked[:, lanes:]
        chosen = jnp.where(mode_lane, picked[0 : 4 * order], 0.0)
        tiled = mm(jnp.concatenate(split(chosen), axis=1), tile) * coef[...]
        rows = [
            jnp.sum(tiled[v * order : (v + 1) * order], axis=0, keepdims=True) for v in range(4)
        ]
        return jnp.concatenate(rows, axis=1), picked[4 * order : 4 * order + 1]

    shrink = (
        (iota((wide_lanes, 4 * corner_rows), 0) // count == (iota((wide_lanes, 4 * corner_rows), 1) & (corner_rows - 1)))
        & (iota((wide_lanes, 4 * corner_rows), 1) < 3 * corner_rows)
    ).astype(bf16)
    middle = iota((count, 4 * corner_rows), 1) // corner_rows == 1

    def lifted(correction):
        spread_out = jnp.where(own_lane, correction, 0.0)
        small = fold(mm(halves(spread_out), shrink))
        high, low = split(small)
        left = jnp.where(middle, low.astype(f32), high.astype(f32)).astype(bf16)
        return [mm(left, lift[d]) for d in range(8)]

    solved, _ = gathered(0)
    added = lifted(solved)
    direct = [base_in[d] + added[4 + d] for d in range(4)]
    product = [base_out[d] + added[d] for d in range(4)]

    def to_owner(k):
        copies = []
        for f in range(2):
            high, low = split(back_values[k][f])
            back_out[k, f] = mm_nt(high, perm[f]) + mm_nt(low, perm[f])
            copies.append(
                remote(
                    back_out.at[k, f],
                    back_in.at[k, f],
                    back_send.at[k, f],
                    back_recv.at[k, f],
                    (west, south)[f],
                )
            )
            copies[-1].start()
        return copies

    back_values = [None, None]
    coarse = restrict([(product[d], d) for d in range(4)])
    sums = pack(
        [
            inner([(residual[f], direct[f]) for f in range(2)]),
            inner([(direct[d], product[d]) for d in range(4)]),
        ]
    )
    zmsg[1] = jnp.concatenate([coarse, sums, jnp.zeros((3, lanes), f32)], axis=0)
    z_start(1)
    back_values[0] = product[2:]
    first_back = to_owner(0)
    applied = []
    for f in range(2):
        first_back[f].wait_recv()
        applied.append((product[f] + back_in[0, f]) * live[f])
        flux_out[f] = halves(applied[f] * weight[f])
    flux = [
        remote(flux_out.at[f], flux_in.at[f], flux_send.at[f], flux_recv.at[f], (east, north)[f])
        for f in range(2)
    ]
    for copy in flux:
        copy.start()
    w_start(1)
    own_flux = [flux_out[f] for f in range(2)]
    for f in range(2):
        flux[f].wait_recv()
        own_flux.append(mm(flux_in[f], perm[f]).astype(bf16))
    flux_product = []
    for d in range(4):
        out = 0.0
        for s in range(4):
            out = out + mm(own_flux[s], blocks[slot[s], slot[d]])
        flux_product.append(fold(out))

    change, sums = gathered(1)
    product_start = unpack(sums, 0)
    curvature = unpack(sums, 1)
    step = product_start / curvature
    step_row = as_row(step)
    solved = solved - jnp.concatenate([step_row] * 4, axis=1) * change
    added = lifted(solved)
    fresh = [
        base_in[d] - step * fold(own_flux[d].astype(f32)) + added[4 + d] for d in range(4)
    ]
    fresh_product = [base_out[d] - step * flux_product[d] + added[d] for d in range(4)]
    residual = [residual[f] - step * applied[f] for f in range(2)]
    zlast[...] = pack(
        [
            inner([(residual[f], fresh[f]) for f in range(2)]),
            inner([(fresh[d], fresh_product[d]) for d in range(4)]),
            inner([(fresh[f], applied[f]) for f in range(2)]),
        ]
    )
    spread(zlast, zlast_buf.at[narrow_at], z_send.at[2], z_recv.at[2], z_peer, narrow_count - 1)
    zlast_buf[narrow_at] = zlast[...]
    back_values[1] = fresh_product[2:]
    second_back = to_owner(1)
    drain(zlast_buf, narrow_count - 1, z_recv.at[2])
    wlast[...] = jnp.sum(zlast_buf[...], axis=0)
    spread(wlast, wlast_buf.at[wide_at], w_send.at[2], w_recv.at[2], w_peer, wide_count - 1)
    wlast_buf[wide_at] = wlast[...]
    fresh_applied = []
    for f in range(2):
        second_back[f].wait_recv()
        fresh_applied.append((fresh_product[f] + back_in[1, f]) * live[f])
    drain(wlast_buf, wide_count - 1, w_recv.at[2])
    sums = jnp.sum(wlast_buf[...], axis=0)
    product_fresh = unpack(sums, 0)
    ratio = product_fresh / product_start
    last_curvature = unpack(sums, 1) + 2.0 * ratio * unpack(sums, 2) + ratio * ratio * curvature
    last_step = product_fresh / last_curvature
    for f in range(2):
        sol_out[:, f, :] = step * direct[f] + last_step * (fresh[f] + ratio * direct[f])
        res_out[:, f, :] = residual[f] - last_step * (fresh_applied[f] + ratio * applied[f])

    for g in range(2):
        drain(zbuf.at[g], narrow_count - 1, z_send.at[g])
        drain(wbuf.at[g], wide_count - 1, w_send.at[g])
    drain(zlast_buf, narrow_count - 1, z_send.at[2])
    drain(wlast_buf, wide_count - 1, w_send.at[2])
    drain(inverses, wide_count - 1, inv_send)
    for copy in fore + flux + first_back + second_back:
        copy.wait_send()


def body(sources, schur, scaling, basis, inverse, sizes, match, slots, corners):
    wide_count = lax.axis_size("wide")
    narrow_count = lax.axis_size("narrow")
    count, width = sources.shape[2], sources.shape[4]
    modes = basis.shape[4]
    order = inverse.shape[1]
    lanes = modes * count
    verts = narrow_count + 1
    msg_rows = -(-(2 * verts + 1) // 8) * 8
    row_slots = jnp.pad(
        jnp.concatenate([corners[:-1], corners[1:]], axis=1),
        ((0, 0), (0, msg_rows - 2 * verts)),
        constant_values=-1,
    ).reshape(1, wide_count * msg_rows)
    vmem = pl.BlockSpec(memory_space=pltpu.VMEM)
    smem = pl.BlockSpec(memory_space=pltpu.SMEM)
    dma = pltpu.SemaphoreType.DMA
    out = jax.ShapeDtypeStruct((count, 2, width), f32)
    corner_rows = 4 * modes
    sol, res = pl.pallas_call(
        kernel,
        out_shape=(out, out),
        in_specs=[smem, smem, smem, vmem, pl.BlockSpec(memory_space=pltpu.HBM)] + [vmem] * 5,
        out_specs=(vmem, vmem),
        scratch_shapes=[
            pltpu.VMEM((4, 4, width, width), bf16),
            pltpu.VMEM((4, 2 * count + 2 * corner_rows, width), bf16),
            pltpu.VMEM((8, 4 * corner_rows, width), bf16),
            pltpu.VMEM((2, width, width), bf16),
            pltpu.VMEM((4 * order + 16, wide_count * msg_rows), bf16),
            pltpu.VMEM((4 * order, lanes), f32),
            pltpu.VMEM((wide_count, order, order), f32),
            pltpu.VMEM((2, 8, lanes), f32),
            pltpu.VMEM((2, narrow_count, 8, lanes), f32),
            pltpu.VMEM((2, msg_rows, lanes), f32),
            pltpu.VMEM((2, wide_count, msg_rows, lanes), f32),
            pltpu.VMEM((1, lanes), f32),
            pltpu.VMEM((narrow_count, 1, lanes), f32),
            pltpu.VMEM((1, lanes), f32),
            pltpu.VMEM((wide_count, 1, lanes), f32),
            pltpu.VMEM((2, 4 * count, width), bf16),
            pltpu.VMEM((2, 4 * count, width), bf16),
            pltpu.VMEM((2, 2 * count, width), bf16),
            pltpu.VMEM((2, 2 * count, width), bf16),
            pltpu.VMEM((2, 2, count, width), f32),
            pltpu.VMEM((2, 2, count, width), f32),
            dma,
            dma((3,)),
            dma((3,)),
            dma((3,)),
            dma((3,)),
            dma((2,)),
            dma((2,)),
            dma((2,)),
            dma((2,)),
            dma((2, 2)),
            dma((2, 2)),
            dma,
            dma,
        ],
        compiler_params=pltpu.CompilerParams(
            collective_id=0, has_side_effects=True, vmem_limit_bytes=48 << 20
        ),
    )(
        sizes[0],
        slots[0],
        corners,
        sources[0, 0],
        schur[0, 0],
        scaling[0, 0],
        basis[0, 0],
        inverse[0],
        match[0, 0],
        row_slots,
    )
    return sol[None, None], res[None, None]


def solution(mesh):
    placed = (
        P("wide", "narrow", None, None, None),
        P("wide", "narrow", None, None),
        P("wide", "narrow", None, None),
        P("wide", "narrow", None, None, None, None),
        P("wide", None, None),
        P("wide", "narrow", None),
        P("wide", "narrow", None, None),
        P("wide", "narrow", None),
        P(),
    )
    return jax.shard_map(
        body,
        mesh=mesh,
        in_specs=placed,
        out_specs=(P("wide", "narrow", None, None, None), P("wide", "narrow", None, None, None)),
        check_vma=False,
    )
```

```python
import jax
import jax.numpy as jnp
from jax import lax
from jax.experimental import pallas as pl
from jax.experimental.pallas import tpu as pltpu
from jax.sharding import PartitionSpec as P

MESH = pl.DeviceIdType.MESH
f32 = jnp.float32
bf16 = jnp.bfloat16
NT = (((1,), (1,)), ((), ()))
EAST, NORTH, WEST, SOUTH = range(4)


def iota(shape, dim):
    return lax.broadcasted_iota(jnp.int32, shape, dim)


def mm(a, b):
    return jnp.dot(a, b, preferred_element_type=f32)


def mm_nt(a, b):
    return lax.dot_general(a, b, NT, preferred_element_type=f32)


def split(x):
    high = x.astype(bf16)
    return high, (x - high.astype(f32)).astype(bf16)


def halves(x):
    return jnp.concatenate(split(x), axis=0)


def fold(x):
    rows = x.shape[0] // 2
    return x[:rows] + x[rows:]


def kernel(
    src_hbm,
    schur,
    scaling_hbm,
    basis_hbm,
    inverse_hbm,
    sizes_hbm,
    match_hbm,
    slots_hbm,
    corners_hbm,
    sol_out,
    res_out,
    src,
    scaling,
    basis,
    inverse,
    match,
    table,
    sizes,
    slots,
    corners,
    blocks,
    faces,
    lift,
    perm,
    pick,
    coef,
    packed,
    inverses,
    zmsg,
    zbuf,
    wmsg,
    wbuf,
    zlast,
    zlast_buf,
    wlast,
    wlast_buf,
    fore_out,
    fore_in,
    flux_out,
    flux_in,
    back_out,
    back_in,
    in_sem,
    load_sem,
    z_send,
    z_recv,
    w_send,
    w_recv,
    fore_send,
    fore_recv,
    flux_send,
    flux_recv,
    back_send,
    back_recv,
    inv_send,
    inv_recv,
):
    wide_count = lax.axis_size("wide")
    narrow_count = lax.axis_size("narrow")
    wide_at = lax.axis_index("wide")
    narrow_at = lax.axis_index("narrow")
    count = src.shape[0]
    width = src.shape[2]
    order = inverse.shape[0]
    half = order // 2
    modes = basis.shape[2]
    capacity = order // modes
    lanes = modes * count
    corner_rows = 4 * modes
    msg_rows = wmsg.shape[1]
    verts = narrow_count + 1

    chips = wide_count // 2
    chip_at = wide_at // 2
    core_at = lax.rem(wide_at, 2)
    team = 2 * narrow_count
    rank = 2 * narrow_at + core_at

    def z_peer(k):
        other = lax.rem(rank + 1 + k, team)
        return (2 * chip_at + lax.rem(other, 2), other // 2)

    def c_peer(k):
        return (2 * lax.rem(chip_at + 1 + k, chips) + core_at, narrow_at)

    def w_peer(k):
        return (lax.rem(wide_at + 1 + k, wide_count), narrow_at)

    east = (lax.rem(wide_at + 1, wide_count), narrow_at)
    west = (lax.rem(wide_at + wide_count - 1, wide_count), narrow_at)
    north = (wide_at, lax.rem(narrow_at + 1, narrow_count))
    south = (wide_at, lax.rem(narrow_at + narrow_count - 1, narrow_count))

    loads = [
        pltpu.make_async_copy(a, b, in_sem.at[i])
        for i, (a, b) in enumerate(
            [
                (sizes_hbm, sizes),
                (src_hbm, src),
                (basis_hbm, basis),
                (scaling_hbm, scaling),
                (inverse_hbm, inverse),
                (match_hbm, match),
                (slots_hbm, slots),
                (corners_hbm, corners),
                (corners_hbm, table),
            ]
        )
    ]
    for copy in loads:
        copy.start()

    barrier = pltpu.get_barrier_semaphore()

    def greet(peer, number):
        def one(k, carry):
            pl.semaphore_signal(barrier, 1, device_id=peer(k), device_id_type=MESH)
            return carry

        lax.fori_loop(0, number, one, 0)

    greet(z_peer, team - 1)
    greet(w_peer, wide_count - 1)

    for s in range(4):
        for t in range(4):
            pltpu.make_async_copy(
                schur.at[pl.ds(s * width, width), pl.ds(t * width, width)],
                blocks.at[s, t],
                load_sem,
            ).start()

    pending = {}

    def remote(a, b, send, recv, device):
        return pltpu.make_async_remote_copy(
            src_ref=a, dst_ref=b, send_sem=send, recv_sem=recv, device_id=device, device_id_type=MESH
        )

    def wait_bytes(ref, number, sem):
        part = ref.at[pl.ds(0, number)]
        pltpu.make_async_copy(part, part, sem).wait()

    def spread(name, a, buf, at, send, recv, peer, number):
        def one(k, carry):
            remote(a, buf.at[at], send, recv, peer(k)).start()
            return carry

        lax.fori_loop(0, number, one, 0)
        pending["send " + name] = lambda: wait_bytes(buf, number, send)
        pending[name] = lambda: wait_bytes(buf, number, recv)

    def single(name, a, b, send, recv, device):
        copy = remote(a, b, send, recv, device)
        copy.start()
        pending["send " + name] = copy.wait_send
        pending[name] = copy.wait_recv

    def arrive(name):
        pending.pop(name)()

    for copy in loads[:4]:
        copy.wait()
    place = iota((1, width), 1)
    live = [(place < sizes[0, f]).astype(f32) for f in range(2)]
    weight = [scaling[f : f + 1, :] * live[f] for f in range(2)]
    residual = [src[:, f, :] * live[f] for f in range(2)]
    scaled = [residual[f] * weight[f] for f in range(2)]
    vec = [[basis[f, e] * live[f] for e in range(2)] for f in range(2)]
    nothing = jnp.zeros((modes, width), f32)

    for f in range(2):
        fore_out[f, 0 : 2 * count, :] = halves(scaled[f])
        fore_out[f, 2 * count : 4 * count, :] = halves(jnp.concatenate(vec[f], axis=0))

    def set_face(d, scaled_parts, ends):
        faces[d, 0 : 2 * count, :] = scaled_parts
        faces[d, 2 * count : 2 * count + 2 * corner_rows, :] = ends

    set_face(
        EAST,
        halves(scaled[0]),
        halves(jnp.concatenate([nothing, nothing, vec[0][0], vec[0][1]], axis=0)),
    )
    set_face(
        NORTH,
        halves(scaled[1]),
        halves(jnp.concatenate([nothing, vec[1][0], nothing, vec[1][1]], axis=0)),
    )

    wide_lanes = 4 * lanes
    grow = ((iota((2 * corner_rows, wide_lanes), 0) & (corner_rows - 1)) == iota((2 * corner_rows, wide_lanes), 1) // count).astype(f32).astype(bf16)
    own_lane = iota((count, wide_lanes), 1) % count == iota((count, wide_lanes), 0)
    own_lane_one = own_lane[:, 0:lanes]

    def restrict(pairs):
        total = 0.0
        for values, d in pairs:
            total = total + mm_nt(
                halves(values), faces[d, 2 * count : 2 * count + 2 * corner_rows, :]
            )
        spread_out = fold(mm(halves(fold(total)), grow))
        row = jnp.sum(jnp.where(own_lane, spread_out, 0.0), axis=0, keepdims=True)
        return jnp.concatenate([row[:, v * lanes : (v + 1) * lanes] for v in range(4)], axis=0)

    def inner(pairs):
        total = 0.0
        for a, b in pairs:
            total = total + jnp.sum(a * b, axis=1, keepdims=True)
        return total

    lane_one = iota((count, lanes), 1)
    row_one = iota((count, lanes), 0)

    def pack(values):
        out = jnp.zeros((count, lanes), f32)
        for g, value in enumerate(values):
            out = out + jnp.where(lane_one == g * count + row_one, value, 0.0)
        return jnp.sum(out, axis=0, keepdims=True)

    def unpack(row, g):
        return jnp.sum(jnp.where(lane_one == g * count + row_one, row, 0.0), axis=1, keepdims=True)

    def as_row(value):
        return jnp.sum(jnp.where(own_lane_one, value, 0.0), axis=0, keepdims=True)

    first = restrict([(residual[0], EAST), (residual[1], NORTH)])
    zmsg[0] = jnp.concatenate([first, jnp.zeros((4, lanes), f32)], axis=0)

    loads[4].wait()
    from_lane = iota((order, lanes), 0)
    to_lane = iota((order, lanes), 1)
    top = ((from_lane == to_lane) & (to_lane < order)).astype(f32).astype(bf16)
    corner = ((from_lane == to_lane - half) & (to_lane >= order)).astype(f32).astype(bf16)
    packed[...] = fold(mm(halves(inverse[0:half, :]), top)) + fold(
        mm(halves(inverse[half:order, :]), corner)
    )

    pl.semaphore_wait(barrier, team - 1 + wide_count - 1)

    def z_start(g):
        spread(f"z{g}", zmsg.at[g], zbuf.at[g], rank, z_send.at[g], z_recv.at[g], z_peer, team - 1)
        zbuf[g, rank] = zmsg[g]

    msg_at = iota((msg_rows, 8 * team), 0)
    from_at = iota((msg_rows, 8 * team), 1)
    from_row = from_at & 7
    from_col = (from_at // 8) & 1
    from_sub = from_at // 16
    goes = (from_col + from_row // 2) * verts + from_sub + (from_row & 1)
    goes = jnp.where(from_row < 4, goes, jnp.where(from_row == 4, 3 * verts, -1))
    merge = (msg_at == goes).astype(f32).astype(bf16)

    def w_start(g):
        arrive(f"z{g}")
        high, low = split(zbuf[g].reshape(8 * team, lanes))
        wmsg[g] = mm(merge, high) + mm(merge, low)
        spread(f"w{g}", wmsg.at[g], wbuf.at[g], chip_at, w_send.at[g], w_recv.at[g], c_peer, chips - 1)
        wbuf[g, chip_at] = wmsg[g]

    z_start(0)
    for f in range(2):
        single(f"fore{f}", fore_out.at[f], fore_in.at[f], fore_send.at[f], fore_recv.at[f], (east, north)[f])
    spread("inv", packed, inverses, wide_at, inv_send, inv_recv, w_peer, wide_count - 1)
    inverses[wide_at] = packed[...]

    for copy in loads[5:]:
        copy.wait()
    for f in range(2):
        perm[f] = (iota((width, width), 0) == match[f : f + 1, :]).astype(f32).astype(bf16)
    vertex = [
        corners[wide_at, narrow_at],
        corners[wide_at, narrow_at + 1],
        corners[wide_at + 1, narrow_at],
        corners[wide_at + 1, narrow_at + 1],
    ]
    owner = [lax.div(v, capacity) for v in vertex]
    place_in = [v - b * capacity for v, b in zip(vertex, owner)]
    total_rows = chips * msg_rows
    row_at = iota((wide_count + 1, total_rows), 1)
    in_msg = row_at % msg_rows
    reach = (
        (iota((wide_count + 1, total_rows), 0) == 2 * (row_at // msg_rows) + in_msg // verts) & (in_msg < 3 * verts)
    ).astype(f32).astype(bf16)
    same = (iota((16, verts), 0) == iota((16, verts), 1)).astype(f32).astype(bf16)
    each = 0.0
    for part in split(table[...].astype(f32)):
        each = each + mm(mm_nt(same, part).astype(bf16), reach)
    row_at = iota((16, total_rows), 1) % msg_rows
    row_slots = jnp.sum(jnp.where(iota((16, total_rows), 0) == row_at % verts, each, 0.0), axis=0, keepdims=True)
    row_slots = jnp.where(iota((1, total_rows), 1) % msg_rows < 3 * verts, row_slots, -1.0)
    for v in range(4):
        wanted = (owner[v] * capacity + iota((order, 1), 0) // modes).astype(f32)
        pick[v * order : (v + 1) * order, :] = (wanted == row_slots).astype(f32).astype(bf16)
    pick[4 * order : 4 * order + 16, :] = (iota((16, total_rows), 1) % msg_rows == 3 * verts).astype(f32).astype(bf16)

    w_start(0)

    for f in range(2):
        arrive(f"fore{f}")
        got = mm(fore_in[f], perm[f])
        parts = []
        for base in (2 * count, 2 * count + 2 * modes):
            low_end = got[base : base + modes]
            high_end = got[base + modes : base + 2 * modes]
            if f == 0:
                parts += [low_end, high_end, nothing, nothing]
            else:
                parts += [low_end, nothing, high_end, nothing]
        set_face(
            WEST + f,
            got[0 : 2 * count].astype(bf16),
            jnp.concatenate(parts, axis=0).astype(bf16),
        )
    pltpu.make_async_copy(blocks, blocks, load_sem).wait()

    slot = [slots[0, d] for d in range(4)]
    base_out = []
    base_in = []
    for d in range(4):
        out = 0.0
        for s in range(4):
            out = out + mm(faces[s], blocks[slot[s], slot[d]])
        base_out.append(out[0:count] + out[count : 2 * count])
        high, low = split(
            out[2 * count : 2 * count + corner_rows]
            + out[2 * count + corner_rows : 2 * count + 2 * corner_rows]
        )
        lift[d, 0:corner_rows] = high
        lift[d, corner_rows : 2 * corner_rows] = high
        lift[d, 2 * corner_rows : 3 * corner_rows] = low
        lift[d, 3 * corner_rows :] = jnp.zeros((corner_rows, width), bf16)
        high = faces[d, 2 * count : 2 * count + corner_rows]
        lift[4 + d, 0:corner_rows] = high
        lift[4 + d, corner_rows : 2 * corner_rows] = high
        lift[4 + d, 2 * corner_rows : 3 * corner_rows] = faces[
            d, 2 * count + corner_rows : 2 * count + 2 * corner_rows
        ]
        lift[4 + d, 3 * corner_rows :] = jnp.zeros((corner_rows, width), bf16)
        base_in.append(
            faces[d, 0:count].astype(f32) + faces[d, count : 2 * count].astype(f32)
        )

    arrive("inv")
    for v in range(4):
        column = place_in[v] * modes + iota((lanes, 2 * lanes), 1) % lanes // count
        column = jnp.where(iota((lanes, 2 * lanes), 1) < lanes, column, column + half)
        take = ((iota((lanes, 2 * lanes), 0) == column) & (place_in[v] * modes >= half)).astype(f32).astype(bf16)
        across = ((iota((order, lanes), 0) % half == place_in[v] * modes + iota((order, lanes), 1) // count) & (place_in[v] * modes < half)).astype(f32).astype(bf16)
        mine = halves(inverses[owner[v]])
        right = fold(mm(mine, take))
        left = lax.dot_general(mine, across, (((0,), (0,)), ((), ())), preferred_element_type=f32)
        coef[v * order : v * order + half, :] = left[0:half] + right[:, 0:lanes]
        coef[v * order + half : (v + 1) * order, :] = left[half:order] + right[:, lanes:]

    tile = ((iota((2 * lanes, lanes), 0) % count) == (iota((2 * lanes, lanes), 1) % count)).astype(f32).astype(bf16)
    mode_lane = iota((4 * order, lanes), 1) // count == (iota((4 * order, lanes), 0) & (modes - 1))

    def gathered(g):
        arrive(f"w{g}")
        parts = jnp.concatenate(split(wbuf[g].reshape(total_rows, lanes)), axis=1)
        picked = mm(pick[...], parts)
        picked = picked[:, 0:lanes] + picked[:, lanes:]
        chosen = jnp.where(mode_lane, picked[0 : 4 * order], 0.0)
        tiled = mm(jnp.concatenate(split(chosen), axis=1), tile) * coef[...]
        rows = [
            jnp.sum(tiled[v * order : (v + 1) * order], axis=0, keepdims=True) for v in range(4)
        ]
        return jnp.concatenate(rows, axis=1), picked[4 * order : 4 * order + 1]

    shrink = (
        (iota((wide_lanes, 4 * corner_rows), 0) // count == (iota((wide_lanes, 4 * corner_rows), 1) & (corner_rows - 1)))
        & (iota((wide_lanes, 4 * corner_rows), 1) < 3 * corner_rows)
    ).astype(f32).astype(bf16)
    middle = iota((count, 4 * corner_rows), 1) // corner_rows == 1

    def lifted(correction):
        spread_out = jnp.where(own_lane, correction, 0.0)
        small = fold(mm(halves(spread_out), shrink))
        high, low = split(small)
        left = jnp.where(middle, low.astype(f32), high.astype(f32)).astype(bf16)
        return [mm(left, lift[d]) for d in range(8)]

    solved, _ = gathered(0)
    added = lifted(solved)
    direct = [base_in[d] + added[4 + d] for d in range(4)]
    product = [base_out[d] + added[d] for d in range(4)]

    def to_owner(k, values):
        for f in range(2):
            high, low = split(values[f])
            back_out[k, f] = mm_nt(high, perm[f]) + mm_nt(low, perm[f])
            single(
                f"back{k}{f}",
                back_out.at[k, f],
                back_in.at[k, f],
                back_send.at[k, f],
                back_recv.at[k, f],
                (west, south)[f],
            )

    coarse = restrict([(product[d], d) for d in range(4)])
    sums = pack(
        [
            inner([(residual[f], direct[f]) for f in range(2)]),
            inner([(direct[d], product[d]) for d in range(4)]),
        ]
    )
    zmsg[1] = jnp.concatenate([coarse, sums, jnp.zeros((3, lanes), f32)], axis=0)
    z_start(1)
    to_owner(0, product[2:])
    applied = []
    for f in range(2):
        arrive(f"back0{f}")
        applied.append((product[f] + back_in[0, f]) * live[f])
        flux_out[f] = halves(applied[f] * weight[f])
        single(f"flux{f}", flux_out.at[f], flux_in.at[f], flux_send.at[f], flux_recv.at[f], (east, north)[f])
    w_start(1)
    own_flux = [flux_out[f] for f in range(2)]
    for f in range(2):
        arrive(f"flux{f}")
        own_flux.append(mm(flux_in[f], perm[f]).astype(bf16))
    flux_product = []
    for d in range(4):
        out = 0.0
        for s in range(4):
            out = out + mm(own_flux[s], blocks[slot[s], slot[d]])
        flux_product.append(fold(out))

    change, sums = gathered(1)
    product_start = unpack(sums, 0)
    curvature = unpack(sums, 1)
    step = product_start / curvature
    step_row = as_row(step)
    solved = solved - jnp.concatenate([step_row] * 4, axis=1) * change
    added = lifted(solved)
    fresh = [
        base_in[d] - step * fold(own_flux[d].astype(f32)) + added[4 + d] for d in range(4)
    ]
    fresh_product = [base_out[d] - step * flux_product[d] + added[d] for d in range(4)]
    residual = [residual[f] - step * applied[f] for f in range(2)]
    zlast[...] = pack(
        [
            inner([(residual[f], fresh[f]) for f in range(2)]),
            inner([(fresh[d], fresh_product[d]) for d in range(4)]),
            inner([(fresh[f], applied[f]) for f in range(2)]),
        ]
    )
    spread("zlast", zlast, zlast_buf, rank, z_send.at[2], z_recv.at[2], z_peer, team - 1)
    zlast_buf[rank] = zlast[...]
    to_owner(1, fresh_product[2:])
    arrive("zlast")
    wlast[...] = jnp.sum(zlast_buf[...], axis=0)
    spread("wlast", wlast, wlast_buf, chip_at, w_send.at[2], w_recv.at[2], c_peer, chips - 1)
    wlast_buf[chip_at] = wlast[...]
    fresh_applied = []
    for f in range(2):
        arrive(f"back1{f}")
        fresh_applied.append((fresh_product[f] + back_in[1, f]) * live[f])
    arrive("wlast")
    sums = jnp.sum(wlast_buf[...], axis=0)
    product_fresh = unpack(sums, 0)
    ratio = product_fresh / product_start
    last_curvature = unpack(sums, 1) + 2.0 * ratio * unpack(sums, 2) + ratio * ratio * curvature
    last_step = product_fresh / last_curvature
    for f in range(2):
        sol_out[:, f, :] = step * direct[f] + last_step * (fresh[f] + ratio * direct[f])
        res_out[:, f, :] = residual[f] - last_step * (fresh_applied[f] + ratio * applied[f])

    for wait in list(pending.values()):
        wait()


def body(sources, schur, scaling, basis, inverse, sizes, match, slots, corners):
    wide_count = lax.axis_size("wide")
    narrow_count = lax.axis_size("narrow")
    count, width = sources.shape[2], sources.shape[4]
    modes = basis.shape[4]
    order = inverse.shape[1]
    lanes = modes * count
    verts = narrow_count + 1
    team = 2 * narrow_count
    chips = wide_count // 2
    msg_rows = -(-(3 * verts + 1) // 8) * 8
    vmem = pl.BlockSpec(memory_space=pltpu.VMEM)
    hbm = pl.BlockSpec(memory_space=pltpu.HBM)
    dma = pltpu.SemaphoreType.DMA
    out = jax.ShapeDtypeStruct((count, 2, width), f32)
    corner_rows = 4 * modes
    sol, res = pl.pallas_call(
        kernel,
        out_shape=(out, out),
        in_specs=[hbm] * 9,
        out_specs=(vmem, vmem),
        scratch_shapes=[
            pltpu.VMEM((count, 2, width), f32),
            pltpu.VMEM((2, width), f32),
            pltpu.VMEM((2, 2, modes, width), f32),
            pltpu.VMEM((order, order), f32),
            pltpu.VMEM((2, width), jnp.int32),
            pltpu.VMEM((wide_count + 1, verts), jnp.int32),
            pltpu.SMEM((1, 2), jnp.int32),
            pltpu.SMEM((1, 4), jnp.int32),
            pltpu.SMEM((wide_count + 1, verts), jnp.int32),
            pltpu.VMEM((4, 4, width, width), bf16),
            pltpu.VMEM((4, 2 * count + 2 * corner_rows, width), bf16),
            pltpu.VMEM((8, 4 * corner_rows, width), bf16),
            pltpu.VMEM((2, width, width), bf16),
            pltpu.VMEM((4 * order + 16, chips * msg_rows), bf16),
            pltpu.VMEM((4 * order, lanes), f32),
            pltpu.VMEM((order // 2, lanes), f32),
            pltpu.VMEM((wide_count, order // 2, lanes), f32),
            pltpu.VMEM((2, 8, lanes), f32),
            pltpu.VMEM((2, team, 8, lanes), f32),
            pltpu.VMEM((2, msg_rows, lanes), f32),
            pltpu.VMEM((2, chips, msg_rows, lanes), f32),
            pltpu.VMEM((1, lanes), f32),
            pltpu.VMEM((team, 1, lanes), f32),
            pltpu.VMEM((1, lanes), f32),
            pltpu.VMEM((chips, 1, lanes), f32),
            pltpu.VMEM((2, 4 * count, width), bf16),
            pltpu.VMEM((2, 4 * count, width), bf16),
            pltpu.VMEM((2, 2 * count, width), bf16),
            pltpu.VMEM((2, 2 * count, width), bf16),
            pltpu.VMEM((2, 2, count, width), f32),
            pltpu.VMEM((2, 2, count, width), f32),
            dma((9,)),
            dma,
            dma((3,)),
            dma((3,)),
            dma((3,)),
            dma((3,)),
            dma((2,)),
            dma((2,)),
            dma((2,)),
            dma((2,)),
            dma((2, 2)),
            dma((2, 2)),
            dma,
            dma,
        ],
        compiler_params=pltpu.CompilerParams(
            collective_id=0, has_side_effects=True, vmem_limit_bytes=48 << 20
        ),
    )(
        sources[0, 0],
        schur[0, 0],
        scaling[0, 0],
        basis[0, 0],
        inverse[0],
        sizes[0],
        match[0, 0],
        slots[0],
        corners,
    )
    return sol[None, None], res[None, None]


def solution(mesh):
    placed = (
        P("wide", "narrow", None, None, None),
        P("wide", "narrow", None, None),
        P("wide", "narrow", None, None),
        P("wide", "narrow", None, None, None, None),
        P("wide", None, None),
        P("wide", "narrow", None),
        P("wide", "narrow", None, None),
        P("wide", "narrow", None),
        P(),
    )
    return jax.shard_map(
        body,
        mesh=mesh,
        in_specs=placed,
        out_specs=(P("wide", "narrow", None, None, None), P("wide", "narrow", None, None, None)),
        check_vma=False,
    )
```

```python
import jax
import jax.numpy as jnp
from jax import lax
from jax.experimental import pallas as pl
from jax.experimental.pallas import tpu as pltpu
from jax.sharding import PartitionSpec as P

MESH = pl.DeviceIdType.MESH
f32 = jnp.float32
bf16 = jnp.bfloat16
NT = (((1,), (1,)), ((), ()))
EAST, NORTH, WEST, SOUTH = range(4)


def iota(shape, dim):
    return lax.broadcasted_iota(jnp.int32, shape, dim)


def quotient(x, n):
    return x >> (n.bit_length() - 1) if n & (n - 1) == 0 else lax.div(x, jnp.int32(n))


def remainder(x, n):
    return x & (n - 1) if n & (n - 1) == 0 else lax.rem(x, jnp.int32(n))


def flags(x):
    return jnp.where(x, 1.0, 0.0).astype(bf16)


def mm(a, b):
    return jnp.dot(a, b, preferred_element_type=f32)


def mm_nt(a, b):
    return lax.dot_general(a, b, NT, preferred_element_type=f32)


def split(x):
    high = x.astype(bf16)
    return high, (x - high.astype(f32)).astype(bf16)


def halves(x):
    return jnp.concatenate(split(x), axis=0)


def fold(x):
    rows = x.shape[0] // 2
    return x[:rows] + x[rows:]


def kernel(
    src_hbm,
    schur,
    scaling_hbm,
    basis_hbm,
    inverse_hbm,
    sizes_hbm,
    match_hbm,
    slots_hbm,
    corners_hbm,
    sol_out,
    res_out,
    src,
    scaling,
    basis,
    inverse,
    match,
    table,
    sizes,
    slots,
    corners,
    blocks,
    faces,
    lift,
    perm,
    pick,
    coef,
    packed,
    inverses,
    zmsg,
    zbuf,
    wmsg,
    wbuf,
    zlast,
    zlast_buf,
    wlast,
    wlast_buf,
    fore_out,
    fore_in,
    flux_out,
    flux_in,
    back_out,
    back_in,
    in_sem,
    load_sem,
    z_send,
    z_recv,
    w_send,
    w_recv,
    fore_send,
    fore_recv,
    flux_send,
    flux_recv,
    back_send,
    back_recv,
    inv_send,
    inv_recv,
):
    wide_count = lax.axis_size("wide")
    narrow_count = lax.axis_size("narrow")
    wide_at = lax.axis_index("wide")
    narrow_at = lax.axis_index("narrow")
    count = src.shape[0]
    width = src.shape[2]
    order = inverse.shape[0]
    half = order // 2
    modes = basis.shape[2]
    capacity = order // modes
    lanes = modes * count
    corner_rows = 4 * modes
    msg_rows = wmsg.shape[1]
    verts = narrow_count + 1

    chips = wide_count // 2
    chip_at = wide_at // 2
    core_at = lax.rem(wide_at, 2)
    team = 2 * narrow_count
    rank = 2 * narrow_at + core_at

    def z_peer(k):
        other = lax.rem(rank + 1 + k, team)
        return (2 * chip_at + lax.rem(other, 2), other // 2)

    def c_peer(k):
        return (2 * lax.rem(chip_at + 1 + k, chips) + core_at, narrow_at)

    east = (lax.rem(wide_at + 1, wide_count), narrow_at)
    west = (lax.rem(wide_at + wide_count - 1, wide_count), narrow_at)
    north = (wide_at, lax.rem(narrow_at + 1, narrow_count))
    south = (wide_at, lax.rem(narrow_at + narrow_count - 1, narrow_count))
    twin = (2 * chip_at + 1 - core_at, narrow_at)

    loads = [
        pltpu.make_async_copy(a, b, in_sem.at[i])
        for i, (a, b) in enumerate(
            [
                (sizes_hbm, sizes),
                (src_hbm, src),
                (basis_hbm, basis),
                (scaling_hbm, scaling),
                (inverse_hbm, inverse),
                (match_hbm, match),
                (slots_hbm, slots),
                (corners_hbm, corners),
                (corners_hbm, table),
            ]
        )
    ]
    for copy in loads:
        copy.start()

    barrier = pltpu.get_barrier_semaphore()

    def greet(peer, number):
        def one(k, carry):
            pl.semaphore_signal(barrier, 1, device_id=peer(k), device_id_type=MESH)
            return carry

        lax.fori_loop(0, number, one, 0)

    greet(z_peer, team - 1)
    greet(c_peer, chips - 1)
    for device in (east, west):
        pl.semaphore_signal(barrier, 1, device_id=device, device_id_type=MESH)

    for s in range(4):
        for t in range(4):
            pltpu.make_async_copy(
                schur.at[pl.ds(s * width, width), pl.ds(t * width, width)],
                blocks.at[s, t],
                load_sem,
            ).start()

    pending = {}

    def remote(a, b, send, recv, device):
        return pltpu.make_async_remote_copy(
            src_ref=a, dst_ref=b, send_sem=send, recv_sem=recv, device_id=device, device_id_type=MESH
        )

    def wait_bytes(ref, number, sem):
        part = ref.at[pl.ds(0, number)]
        pltpu.make_async_copy(part, part, sem).wait()

    def spread(name, a, buf, at, send, recv, peer, number):
        def one(k, carry):
            remote(a, buf.at[at], send, recv, peer(k)).start()
            return carry

        lax.fori_loop(0, number, one, 0)
        pending["send " + name] = lambda: wait_bytes(buf, number, send)
        pending[name] = lambda: wait_bytes(buf, number, recv)

    def single(name, a, b, send, recv, device):
        copy = remote(a, b, send, recv, device)
        copy.start()
        pending["send " + name] = copy.wait_send
        pending[name] = copy.wait_recv

    def arrive(name):
        pending.pop(name)()

    for copy in loads[:4]:
        copy.wait()
    place = iota((1, width), 1)
    live = [(place < sizes[0, f]).astype(f32) for f in range(2)]
    weight = [scaling[f : f + 1, :] * live[f] for f in range(2)]
    residual = [src[:, f, :] * live[f] for f in range(2)]
    scaled = [residual[f] * weight[f] for f in range(2)]
    vec = [[basis[f, e] * live[f] for e in range(2)] for f in range(2)]
    nothing = jnp.zeros((modes, width), f32)

    for f in range(2):
        fore_out[f, 0 : 2 * count, :] = halves(scaled[f])
        fore_out[f, 2 * count : 4 * count, :] = halves(jnp.concatenate(vec[f], axis=0))

    def set_face(d, scaled_parts, ends):
        faces[d, 0 : 2 * count, :] = scaled_parts
        faces[d, 2 * count : 2 * count + 2 * corner_rows, :] = ends

    set_face(
        EAST,
        halves(scaled[0]),
        halves(jnp.concatenate([nothing, nothing, vec[0][0], vec[0][1]], axis=0)),
    )
    set_face(
        NORTH,
        halves(scaled[1]),
        halves(jnp.concatenate([nothing, vec[1][0], nothing, vec[1][1]], axis=0)),
    )

    wide_lanes = 4 * lanes
    grow = flags(remainder(iota((2 * corner_rows, wide_lanes), 0), corner_rows) == quotient(iota((2 * corner_rows, wide_lanes), 1), count))
    own_lane = remainder(iota((count, wide_lanes), 1), count) == iota((count, wide_lanes), 0)
    own_lane_one = own_lane[:, 0:lanes]

    def restrict(pairs):
        total = 0.0
        for values, d in pairs:
            total = total + mm_nt(
                halves(values), faces[d, 2 * count : 2 * count + 2 * corner_rows, :]
            )
        spread_out = fold(mm(halves(fold(total)), grow))
        row = jnp.sum(jnp.where(own_lane, spread_out, 0.0), axis=0, keepdims=True)
        return jnp.concatenate([row[:, v * lanes : (v + 1) * lanes] for v in range(4)], axis=0)

    def inner(pairs):
        total = 0.0
        for a, b in pairs:
            total = total + jnp.sum(a * b, axis=1, keepdims=True)
        return total

    lane_one = iota((count, lanes), 1)
    row_one = iota((count, lanes), 0)

    def pack(values):
        out = jnp.zeros((count, lanes), f32)
        for g, value in enumerate(values):
            out = out + jnp.where(lane_one == g * count + row_one, value, 0.0)
        return jnp.sum(out, axis=0, keepdims=True)

    def unpack(row, g):
        return jnp.sum(jnp.where(lane_one == g * count + row_one, row, 0.0), axis=1, keepdims=True)

    def as_row(value):
        return jnp.sum(jnp.where(own_lane_one, value, 0.0), axis=0, keepdims=True)

    first = restrict([(residual[0], EAST), (residual[1], NORTH)])
    zmsg[0] = jnp.concatenate([first, jnp.zeros((4, lanes), f32)], axis=0)

    loads[4].wait()
    from_lane = iota((order, lanes), 0)
    to_lane = iota((order, lanes), 1)
    top = flags((from_lane == to_lane) & (to_lane < order))
    corner = flags((from_lane == to_lane - half) & (to_lane >= order))
    packed[...] = fold(mm(halves(inverse[0:half, :]), top)) + fold(
        mm(halves(inverse[half:order, :]), corner)
    )

    msg_at = iota((msg_rows, 8 * team), 0)
    from_at = iota((msg_rows, 8 * team), 1)
    from_row = from_at & 7
    from_col = (from_at >> 3) & 1
    from_sub = from_at >> 4
    goes = (from_col + (from_row >> 1)) * verts + from_sub + (from_row & 1)
    goes = jnp.where(from_row < 4, goes, jnp.where(from_row == 4, 3 * verts, -1))
    merge = flags(msg_at == goes)

    pl.semaphore_wait(barrier, team - 1 + chips - 1 + 2)

    def z_start(g):
        spread(f"z{g}", zmsg.at[g], zbuf.at[g], rank, z_send.at[g], z_recv.at[g], z_peer, team - 1)
        zbuf[g, rank] = zmsg[g]

    def w_start(g):
        arrive(f"z{g}")
        high, low = split(zbuf[g].reshape(8 * team, lanes))
        wmsg[g] = mm(merge, high) + mm(merge, low)
        spread(f"w{g}", wmsg.at[g], wbuf.at[g], chip_at, w_send.at[g], w_recv.at[g], c_peer, chips - 1)
        wbuf[g, chip_at] = wmsg[g]

    z_start(0)
    for f in range(2):
        single(f"fore{f}", fore_out.at[f], fore_in.at[f], fore_send.at[f], fore_recv.at[f], (east, north)[f])
    spread("inv", packed, inverses.at[core_at], chip_at, inv_send.at[0], inv_recv.at[0], c_peer, chips - 1)
    inverses[core_at, chip_at] = packed[...]

    for copy in loads[5:]:
        copy.wait()
    for f in range(2):
        perm[f] = flags(iota((width, width), 0) == match[f : f + 1, :])
    vertex = [
        corners[narrow_at, wide_at],
        corners[narrow_at + 1, wide_at],
        corners[narrow_at, wide_at + 1],
        corners[narrow_at + 1, wide_at + 1],
    ]
    owner = [lax.div(v, capacity) for v in vertex]
    place_in = [v - b * capacity for v, b in zip(vertex, owner)]
    total_rows = chips * msg_rows
    in_msg = remainder(iota((1, total_rows), 1), msg_rows)
    in_col = (in_msg >= verts).astype(jnp.int32) + (in_msg >= 2 * verts).astype(jnp.int32)
    column = 2 * quotient(iota((1, total_rows), 1), msg_rows) + in_col
    column = jnp.where(in_msg < 3 * verts, column, -1)
    reach = flags(iota((wide_count + 1, total_rows), 0) == column)
    each = 0.0
    for part in split(table[...].astype(f32)):
        each = each + mm(part, reach)
    row_slots = jnp.sum(jnp.where(iota((verts, total_rows), 0) == in_msg - verts * in_col, each, 0.0), axis=0, keepdims=True)
    row_slots = jnp.where(in_msg < 3 * verts, row_slots, -1.0)
    for v in range(4):
        wanted = (owner[v] * capacity + quotient(iota((order, 1), 0), modes)).astype(f32)
        pick[v * order : (v + 1) * order, :] = flags(wanted == row_slots)
    pick[4 * order : 4 * order + 16, :] = flags(jnp.broadcast_to(in_msg, (16, total_rows)) == 3 * verts)

    w_start(0)

    def relay():
        arrive("inv")
        half_held = inverses.at[core_at]
        single("relay", half_held, half_held, inv_send.at[1], inv_recv.at[1], twin)


    for f in range(2):
        arrive(f"fore{f}")
        got = mm(fore_in[f], perm[f])
        parts = []
        for base in (2 * count, 2 * count + 2 * modes):
            low_end = got[base : base + modes]
            high_end = got[base + modes : base + 2 * modes]
            if f == 0:
                parts += [low_end, high_end, nothing, nothing]
            else:
                parts += [low_end, nothing, high_end, nothing]
        set_face(
            WEST + f,
            got[0 : 2 * count].astype(bf16),
            jnp.concatenate(parts, axis=0).astype(bf16),
        )
    pltpu.make_async_copy(blocks, blocks, load_sem).wait()
    relay()

    slot = [slots[0, d] for d in range(4)]
    base_out = []
    base_in = []
    for d in range(4):
        out = 0.0
        for s in range(4):
            out = out + mm(faces[s], blocks[slot[s], slot[d]])
        base_out.append(out[0:count] + out[count : 2 * count])
        high, low = split(
            out[2 * count : 2 * count + corner_rows]
            + out[2 * count + corner_rows : 2 * count + 2 * corner_rows]
        )
        lift[d, 0:corner_rows] = high
        lift[d, corner_rows : 2 * corner_rows] = high
        lift[d, 2 * corner_rows : 3 * corner_rows] = low
        lift[d, 3 * corner_rows :] = jnp.zeros((corner_rows, width), bf16)
        high = faces[d, 2 * count : 2 * count + corner_rows]
        lift[4 + d, 0:corner_rows] = high
        lift[4 + d, corner_rows : 2 * corner_rows] = high
        lift[4 + d, 2 * corner_rows : 3 * corner_rows] = faces[
            d, 2 * count + corner_rows : 2 * count + 2 * corner_rows
        ]
        lift[4 + d, 3 * corner_rows :] = jnp.zeros((corner_rows, width), bf16)
        base_in.append(
            faces[d, 0:count].astype(f32) + faces[d, count : 2 * count].astype(f32)
        )

    arrive("relay")
    lane_at = iota((lanes, 2 * lanes), 1)
    lane_mode = quotient(remainder(lane_at, lanes), count)
    base_lane = iota((lanes, 2 * lanes), 0) - lane_mode - jnp.where(lane_at < lanes, 0, half)
    row_at = iota((order, lanes), 0)
    base_row = jnp.where(row_at < half, row_at, row_at - half) - quotient(iota((order, lanes), 1), count)
    for v in range(4):
        first_at = place_in[v] * modes
        take = flags(base_lane == jnp.where(first_at >= half, first_at, -order * lanes))
        across = flags(base_row == jnp.where(first_at < half, first_at, -order * lanes))
        mine = halves(inverses[lax.rem(owner[v], 2), lax.div(owner[v], 2)])
        right = fold(mm(mine, take))
        left = lax.dot_general(mine, across, (((0,), (0,)), ((), ())), preferred_element_type=f32)
        coef[v * order : v * order + half, :] = left[0:half] + right[:, 0:lanes]
        coef[v * order + half : (v + 1) * order, :] = left[half:order] + right[:, lanes:]

    tile = flags(remainder(iota((2 * lanes, lanes), 0), count) == remainder(iota((2 * lanes, lanes), 1), count))
    mode_lane = quotient(iota((4 * order, lanes), 1), count) == remainder(iota((4 * order, lanes), 0), modes)

    def gathered(g):
        arrive(f"w{g}")
        parts = jnp.concatenate(split(wbuf[g].reshape(total_rows, lanes)), axis=1)
        picked = mm(pick[...], parts)
        picked = picked[:, 0:lanes] + picked[:, lanes:]
        chosen = jnp.where(mode_lane, picked[0 : 4 * order], 0.0)
        tiled = mm(jnp.concatenate(split(chosen), axis=1), tile) * coef[...]
        rows = [
            jnp.sum(tiled[v * order : (v + 1) * order], axis=0, keepdims=True) for v in range(4)
        ]
        return jnp.concatenate(rows, axis=1), picked[4 * order : 4 * order + 1]

    to_small = iota((wide_lanes, 4 * corner_rows), 1)
    shrink = flags(
        (quotient(iota((wide_lanes, 4 * corner_rows), 0), count) == remainder(to_small, corner_rows))
        & (to_small < 3 * corner_rows)
    )
    middle = quotient(iota((count, 4 * corner_rows), 1), corner_rows) == 1

    def lifted(correction):
        spread_out = jnp.where(own_lane, correction, 0.0)
        small = fold(mm(halves(spread_out), shrink))
        high, low = split(small)
        left = jnp.where(middle, low.astype(f32), high.astype(f32)).astype(bf16)
        return [mm(left, lift[d]) for d in range(8)]

    solved, _ = gathered(0)
    added = lifted(solved)
    direct = [base_in[d] + added[4 + d] for d in range(4)]
    product = [base_out[d] + added[d] for d in range(4)]

    def to_owner(k, values):
        for f in range(2):
            high, low = split(values[f])
            back_out[k, f] = mm_nt(high, perm[f]) + mm_nt(low, perm[f])
            single(
                f"back{k}{f}",
                back_out.at[k, f],
                back_in.at[k, f],
                back_send.at[k, f],
                back_recv.at[k, f],
                (west, south)[f],
            )

    coarse = restrict([(product[d], d) for d in range(4)])
    sums = pack(
        [
            inner([(residual[f], direct[f]) for f in range(2)]),
            inner([(direct[d], product[d]) for d in range(4)]),
        ]
    )
    zmsg[1] = jnp.concatenate([coarse, sums, jnp.zeros((3, lanes), f32)], axis=0)
    z_start(1)
    to_owner(0, product[2:])
    applied = []
    for f in range(2):
        arrive(f"back0{f}")
        applied.append((product[f] + back_in[0, f]) * live[f])
        flux_out[f] = halves(applied[f] * weight[f])
        single(f"flux{f}", flux_out.at[f], flux_in.at[f], flux_send.at[f], flux_recv.at[f], (east, north)[f])
    w_start(1)
    own_flux = [flux_out[f] for f in range(2)]
    for f in range(2):
        arrive(f"flux{f}")
        own_flux.append(mm(flux_in[f], perm[f]).astype(bf16))
    flux_product = []
    for d in range(4):
        out = 0.0
        for s in range(4):
            out = out + mm(own_flux[s], blocks[slot[s], slot[d]])
        flux_product.append(fold(out))

    change, sums = gathered(1)
    product_start = unpack(sums, 0)
    curvature = unpack(sums, 1)
    step = product_start / curvature
    step_row = as_row(step)
    solved = solved - jnp.concatenate([step_row] * 4, axis=1) * change
    added = lifted(solved)
    fresh = [
        base_in[d] - step * fold(own_flux[d].astype(f32)) + added[4 + d] for d in range(4)
    ]
    fresh_product = [base_out[d] - step * flux_product[d] + added[d] for d in range(4)]
    residual = [residual[f] - step * applied[f] for f in range(2)]
    zlast[...] = pack(
        [
            inner([(residual[f], fresh[f]) for f in range(2)]),
            inner([(fresh[d], fresh_product[d]) for d in range(4)]),
            inner([(fresh[f], applied[f]) for f in range(2)]),
        ]
    )
    spread("zlast", zlast, zlast_buf, rank, z_send.at[2], z_recv.at[2], z_peer, team - 1)
    zlast_buf[rank] = zlast[...]
    to_owner(1, fresh_product[2:])
    arrive("zlast")
    wlast[...] = jnp.sum(zlast_buf[...], axis=0)
    spread("wlast", wlast, wlast_buf, chip_at, w_send.at[2], w_recv.at[2], c_peer, chips - 1)
    wlast_buf[chip_at] = wlast[...]
    fresh_applied = []
    for f in range(2):
        arrive(f"back1{f}")
        fresh_applied.append((fresh_product[f] + back_in[1, f]) * live[f])
    arrive("wlast")
    sums = jnp.sum(wlast_buf[...], axis=0)
    product_fresh = unpack(sums, 0)
    ratio = product_fresh / product_start
    last_curvature = unpack(sums, 1) + 2.0 * ratio * unpack(sums, 2) + ratio * ratio * curvature
    last_step = product_fresh / last_curvature
    for f in range(2):
        sol_out[:, f, :] = step * direct[f] + last_step * (fresh[f] + ratio * direct[f])
        res_out[:, f, :] = residual[f] - last_step * (fresh_applied[f] + ratio * applied[f])

    for wait in list(pending.values()):
        wait()


def body(sources, schur, scaling, basis, inverse, sizes, match, slots, corners):
    wide_count = lax.axis_size("wide")
    narrow_count = lax.axis_size("narrow")
    count, width = sources.shape[2], sources.shape[4]
    modes = basis.shape[4]
    order = inverse.shape[1]
    lanes = modes * count
    verts = narrow_count + 1
    team = 2 * narrow_count
    chips = wide_count // 2
    msg_rows = -(-(3 * verts + 1) // 8) * 8
    vmem = pl.BlockSpec(memory_space=pltpu.VMEM)
    hbm = pl.BlockSpec(memory_space=pltpu.HBM)
    dma = pltpu.SemaphoreType.DMA
    out = jax.ShapeDtypeStruct((count, 2, width), f32)
    corner_rows = 4 * modes
    sol, res = pl.pallas_call(
        kernel,
        out_shape=(out, out),
        in_specs=[hbm] * 9,
        out_specs=(vmem, vmem),
        scratch_shapes=[
            pltpu.VMEM((count, 2, width), f32),
            pltpu.VMEM((2, width), f32),
            pltpu.VMEM((2, 2, modes, width), f32),
            pltpu.VMEM((order, order), f32),
            pltpu.VMEM((2, width), jnp.int32),
            pltpu.VMEM((verts, wide_count + 1), jnp.int32),
            pltpu.SMEM((1, 2), jnp.int32),
            pltpu.SMEM((1, 4), jnp.int32),
            pltpu.SMEM((verts, wide_count + 1), jnp.int32),
            pltpu.VMEM((4, 4, width, width), bf16),
            pltpu.VMEM((4, 2 * count + 2 * corner_rows, width), bf16),
            pltpu.VMEM((8, 4 * corner_rows, width), bf16),
            pltpu.VMEM((2, width, width), bf16),
            pltpu.VMEM((4 * order + 16, chips * msg_rows), bf16),
            pltpu.VMEM((4 * order, lanes), f32),
            pltpu.VMEM((order // 2, lanes), f32),
            pltpu.VMEM((2, chips, order // 2, lanes), f32),
            pltpu.VMEM((2, 8, lanes), f32),
            pltpu.VMEM((2, team, 8, lanes), f32),
            pltpu.VMEM((2, msg_rows, lanes), f32),
            pltpu.VMEM((2, chips, msg_rows, lanes), f32),
            pltpu.VMEM((1, lanes), f32),
            pltpu.VMEM((team, 1, lanes), f32),
            pltpu.VMEM((1, lanes), f32),
            pltpu.VMEM((chips, 1, lanes), f32),
            pltpu.VMEM((2, 4 * count, width), bf16),
            pltpu.VMEM((2, 4 * count, width), bf16),
            pltpu.VMEM((2, 2 * count, width), bf16),
            pltpu.VMEM((2, 2 * count, width), bf16),
            pltpu.VMEM((2, 2, count, width), f32),
            pltpu.VMEM((2, 2, count, width), f32),
            dma((9,)),
            dma,
            dma((3,)),
            dma((3,)),
            dma((3,)),
            dma((3,)),
            dma((2,)),
            dma((2,)),
            dma((2,)),
            dma((2,)),
            dma((2, 2)),
            dma((2, 2)),
            dma((2,)),
            dma((2,)),
        ],
        compiler_params=pltpu.CompilerParams(
            collective_id=0, has_side_effects=True, vmem_limit_bytes=48 << 20
        ),
    )(
        *(
            pltpu.with_memory_space_constraint(x, pltpu.HBM)
            for x in (
                sources[0, 0],
                schur[0, 0],
                scaling[0, 0],
                basis[0, 0],
                inverse[0],
                sizes[0],
                match[0, 0],
                slots[0],
                corners.T,
            )
        )
    )
    return sol[None, None], res[None, None]


def solution(mesh):
    placed = (
        P("wide", "narrow", None, None, None),
        P("wide", "narrow", None, None),
        P("wide", "narrow", None, None),
        P("wide", "narrow", None, None, None, None),
        P("wide", None, None),
        P("wide", "narrow", None),
        P("wide", "narrow", None, None),
        P("wide", "narrow", None),
        P(),
    )
    return jax.shard_map(
        body,
        mesh=mesh,
        in_specs=placed,
        out_specs=(P("wide", "narrow", None, None, None), P("wide", "narrow", None, None, None)),
        check_vma=False,
    )
```

```python
import jax
import jax.numpy as jnp
from jax import lax
from jax.experimental import pallas as pl
from jax.experimental.pallas import tpu as pltpu
from jax.sharding import PartitionSpec as P

MESH = pl.DeviceIdType.MESH
f32 = jnp.float32
bf16 = jnp.bfloat16
NT = (((1,), (1,)), ((), ()))
EAST, NORTH, WEST, SOUTH = range(4)


def iota(shape, dim):
    return lax.broadcasted_iota(jnp.int32, shape, dim)


def quotient(x, n):
    return x >> (n.bit_length() - 1) if n & (n - 1) == 0 else lax.div(x, jnp.int32(n))


def remainder(x, n):
    return x & (n - 1) if n & (n - 1) == 0 else lax.rem(x, jnp.int32(n))


def flags(x):
    return jnp.where(x, 1.0, 0.0).astype(bf16)


def mm(a, b):
    return jnp.dot(a, b, preferred_element_type=f32)


def mm_nt(a, b):
    return lax.dot_general(a, b, NT, preferred_element_type=f32)


def split(x):
    high = x.astype(bf16)
    return high, (x - high.astype(f32)).astype(bf16)


def halves(x):
    return jnp.concatenate(split(x), axis=0)


def fold(x):
    rows = x.shape[0] // 2
    return x[:rows] + x[rows:]


def kernel(
    src_hbm,
    schur,
    scaling_hbm,
    basis_hbm,
    inverse_hbm,
    sizes_hbm,
    match_hbm,
    slots_hbm,
    corners_hbm,
    sol_out,
    res_out,
    src,
    scaling,
    basis,
    inverse,
    match,
    table,
    sizes,
    slots,
    corners,
    blocks,
    faces,
    lift,
    perm,
    pick,
    coef,
    packed,
    inverses,
    zmsg,
    zbuf,
    wmsg,
    wbuf,
    zlast,
    zlast_buf,
    wlast,
    wlast_buf,
    fore_out,
    fore_in,
    flux_out,
    flux_in,
    back_out,
    back_in,
    in_sem,
    load_sem,
    z_send,
    z_recv,
    w_send,
    w_recv,
    fore_send,
    fore_recv,
    flux_send,
    flux_recv,
    back_send,
    back_recv,
    inv_send,
    inv_recv,
):
    wide_count = lax.axis_size("wide")
    narrow_count = lax.axis_size("narrow")
    wide_at = lax.axis_index("wide")
    narrow_at = lax.axis_index("narrow")
    count = src.shape[0]
    width = src.shape[2]
    order = inverse.shape[0]
    half = order // 2
    modes = basis.shape[2]
    capacity = order // modes
    lanes = modes * count
    corner_rows = 4 * modes
    msg_rows = wmsg.shape[1]
    verts = narrow_count + 1

    chips = wide_count // 2
    chip_at = wide_at // 2
    core_at = lax.rem(wide_at, 2)
    team = 2 * narrow_count
    rank = 2 * narrow_at + core_at

    side = 4
    ring = chips // side

    def around(t, size):
        return size // 2 + lax.div(t, 2) * (1 - lax.rem(t, 2)) - lax.div(t + 1, 2) * lax.rem(t, 2)

    def z_peer(k):
        core = lax.rem(core_at + 1 + lax.rem(k, 2), 2)
        return (2 * chip_at + core, lax.rem(narrow_at + around(lax.div(k, 2), narrow_count), narrow_count))

    def c_peer(k):
        x = lax.rem(lax.div(chip_at, side) + around(lax.div(k, side), ring), ring)
        y = lax.rem(chip_at + around(lax.rem(k, side), side), side)
        return (2 * (x * side + y) + core_at, narrow_at)

    east = (lax.rem(wide_at + 1, wide_count), narrow_at)
    west = (lax.rem(wide_at + wide_count - 1, wide_count), narrow_at)
    north = (wide_at, lax.rem(narrow_at + 1, narrow_count))
    south = (wide_at, lax.rem(narrow_at + narrow_count - 1, narrow_count))
    twin = (2 * chip_at + 1 - core_at, narrow_at)

    barrier = pltpu.get_barrier_semaphore()

    def greet(peer, number):
        def one(k, carry):
            pl.semaphore_signal(barrier, 1, device_id=peer(k), device_id_type=MESH)
            return carry

        lax.fori_loop(0, number, one, 0)

    greet(z_peer, team - 1)
    greet(c_peer, chips - 1)
    for device in (east, west):
        pl.semaphore_signal(barrier, 1, device_id=device, device_id_type=MESH)

    loads = [
        pltpu.make_async_copy(a, b, in_sem.at[i])
        for i, (a, b) in enumerate(
            [
                (sizes_hbm, sizes),
                (src_hbm, src),
                (basis_hbm, basis),
                (scaling_hbm, scaling),
                (inverse_hbm, inverse),
                (match_hbm, match),
                (slots_hbm, slots),
                (corners_hbm, corners),
                (corners_hbm, table),
            ]
        )
    ]
    for copy in loads:
        copy.start()

    for s in range(4):
        for t in range(4):
            pltpu.make_async_copy(
                schur.at[pl.ds(s * width, width), pl.ds(t * width, width)],
                blocks.at[s, t],
                load_sem,
            ).start()

    pending = {}

    def remote(a, b, send, recv, device):
        return pltpu.make_async_remote_copy(
            src_ref=a, dst_ref=b, send_sem=send, recv_sem=recv, device_id=device, device_id_type=MESH
        )

    def wait_bytes(ref, number, sem):
        part = ref.at[pl.ds(0, number)]
        pltpu.make_async_copy(part, part, sem).wait()

    def spread(name, a, buf, at, send, recv, peer, number):
        def one(k, carry):
            remote(a, buf.at[at], send, recv, peer(k)).start()
            return carry

        lax.fori_loop(0, number, one, 0)
        pending["send " + name] = lambda: wait_bytes(buf, number, send)
        pending[name] = lambda: wait_bytes(buf, number, recv)

    def single(name, a, b, send, recv, device):
        copy = remote(a, b, send, recv, device)
        copy.start()
        pending["send " + name] = copy.wait_send
        pending[name] = copy.wait_recv

    def arrive(name):
        pending.pop(name)()

    for copy in loads[:4]:
        copy.wait()
    place = iota((1, width), 1)
    live = [(place < sizes[0, f]).astype(f32) for f in range(2)]
    weight = [scaling[f : f + 1, :] * live[f] for f in range(2)]
    residual = [src[:, f, :] * live[f] for f in range(2)]
    scaled = [residual[f] * weight[f] for f in range(2)]
    vec = [[basis[f, e] * live[f] for e in range(2)] for f in range(2)]
    nothing = jnp.zeros((modes, width), f32)

    for f in range(2):
        fore_out[f, 0 : 2 * count, :] = halves(scaled[f])
        fore_out[f, 2 * count : 4 * count, :] = halves(jnp.concatenate(vec[f], axis=0))

    def set_face(d, scaled_parts, ends):
        faces[d, 0 : 2 * count, :] = scaled_parts
        faces[d, 2 * count : 2 * count + 2 * corner_rows, :] = ends

    set_face(
        EAST,
        halves(scaled[0]),
        halves(jnp.concatenate([nothing, nothing, vec[0][0], vec[0][1]], axis=0)),
    )
    set_face(
        NORTH,
        halves(scaled[1]),
        halves(jnp.concatenate([nothing, vec[1][0], nothing, vec[1][1]], axis=0)),
    )

    wide_lanes = 4 * lanes
    grow = flags(remainder(iota((2 * corner_rows, wide_lanes), 0), corner_rows) == quotient(iota((2 * corner_rows, wide_lanes), 1), count))
    own_lane = remainder(iota((count, wide_lanes), 1), count) == iota((count, wide_lanes), 0)
    own_lane_one = own_lane[:, 0:lanes]

    def project(pairs):
        total = 0.0
        for values, d in pairs:
            total = total + mm_nt(
                halves(values), faces[d, 2 * count : 2 * count + 2 * corner_rows, :]
            )
        return fold(total)

    def corner_rows_of(projected):
        spread_out = fold(mm(halves(projected), grow))
        row = jnp.sum(jnp.where(own_lane, spread_out, 0.0), axis=0, keepdims=True)
        return jnp.concatenate([row[:, v * lanes : (v + 1) * lanes] for v in range(4)], axis=0)

    def across_lanes(a, b):
        return jnp.sum(a[:, 0 : 2 * corner_rows] * b, axis=1, keepdims=True)

    def inner(pairs):
        total = 0.0
        for a, b in pairs:
            total = total + jnp.sum(a * b, axis=1, keepdims=True)
        return total

    lane_one = iota((count, lanes), 1)
    row_one = iota((count, lanes), 0)

    def pack(values):
        out = jnp.zeros((count, lanes), f32)
        for g, value in enumerate(values):
            out = out + jnp.where(lane_one == g * count + row_one, value, 0.0)
        return jnp.sum(out, axis=0, keepdims=True)

    def unpack(row, g):
        return jnp.sum(jnp.where(lane_one == g * count + row_one, row, 0.0), axis=1, keepdims=True)

    def as_row(value):
        return jnp.sum(jnp.where(own_lane_one, value, 0.0), axis=0, keepdims=True)

    start_coarse = project([(residual[0], EAST), (residual[1], NORTH)])
    first = corner_rows_of(start_coarse)
    zmsg[0] = jnp.concatenate([first, jnp.zeros((4, lanes), f32)], axis=0)

    loads[4].wait()
    from_lane = iota((order, lanes), 0)
    to_lane = iota((order, lanes), 1)
    top = flags((from_lane == to_lane) & (to_lane < order))
    corner = flags((from_lane == to_lane - half) & (to_lane >= order))
    packed[...] = fold(mm(halves(inverse[0:half, :]), top)) + fold(
        mm(halves(inverse[half:order, :]), corner)
    )

    msg_at = iota((msg_rows, 8 * team), 0)
    from_at = iota((msg_rows, 8 * team), 1)
    from_row = from_at & 7
    from_col = (from_at >> 3) & 1
    from_sub = from_at >> 4
    goes = (from_col + (from_row >> 1)) * verts + from_sub + (from_row & 1)
    goes = jnp.where(from_row < 4, goes, jnp.where(from_row == 4, 3 * verts, -1))
    merge = flags(msg_at == goes)

    pl.semaphore_wait(barrier, team - 1 + chips - 1 + 2)

    def z_start(g):
        spread(f"z{g}", zmsg.at[g], zbuf.at[g], rank, z_send.at[g], z_recv.at[g], z_peer, team - 1)
        zbuf[g, rank] = zmsg[g]

    def w_start(g):
        arrive(f"z{g}")
        high, low = split(zbuf[g].reshape(8 * team, lanes))
        wmsg[g] = mm(merge, high) + mm(merge, low)
        spread(f"w{g}", wmsg.at[g], wbuf.at[g], chip_at, w_send.at[g], w_recv.at[g], c_peer, chips - 1)
        wbuf[g, chip_at] = wmsg[g]

    z_start(0)
    for f in range(2):
        single(f"fore{f}", fore_out.at[f], fore_in.at[f], fore_send.at[f], fore_recv.at[f], (east, north)[f])
    spread("inv", packed, inverses.at[core_at], chip_at, inv_send.at[0], inv_recv.at[0], c_peer, chips - 1)
    inverses[core_at, chip_at] = packed[...]

    for copy in loads[5:]:
        copy.wait()
    for f in range(2):
        perm[f] = flags(iota((width, width), 0) == match[f : f + 1, :])
    vertex = [
        corners[narrow_at, wide_at],
        corners[narrow_at + 1, wide_at],
        corners[narrow_at, wide_at + 1],
        corners[narrow_at + 1, wide_at + 1],
    ]
    owner = [lax.div(v, capacity) for v in vertex]
    place_in = [v - b * capacity for v, b in zip(vertex, owner)]
    total_rows = chips * msg_rows
    in_msg = remainder(iota((1, total_rows), 1), msg_rows)
    in_col = (in_msg >= verts).astype(jnp.int32) + (in_msg >= 2 * verts).astype(jnp.int32)
    column = 2 * quotient(iota((1, total_rows), 1), msg_rows) + in_col
    column = jnp.where(in_msg < 3 * verts, column, -1)
    reach = flags(iota((wide_count + 1, total_rows), 0) == column)
    each = 0.0
    for part in split(table[...].astype(f32)):
        each = each + mm(part, reach)
    row_slots = jnp.sum(jnp.where(iota((verts, total_rows), 0) == in_msg - verts * in_col, each, 0.0), axis=0, keepdims=True)
    row_slots = jnp.where(in_msg < 3 * verts, row_slots, -1.0)
    for v in range(4):
        wanted = (owner[v] * capacity + quotient(iota((order, 1), 0), modes)).astype(f32)
        pick[v * order : (v + 1) * order, :] = flags(wanted == row_slots)
    pick[4 * order : 4 * order + 16, :] = flags(jnp.broadcast_to(in_msg, (16, total_rows)) == 3 * verts)

    w_start(0)

    def relay():
        arrive("inv")
        half_held = inverses.at[core_at]
        single("relay", half_held, half_held, inv_send.at[1], inv_recv.at[1], twin)


    for f in range(2):
        arrive(f"fore{f}")
        got = mm(fore_in[f], perm[f])
        parts = []
        for base in (2 * count, 2 * count + 2 * modes):
            low_end = got[base : base + modes]
            high_end = got[base + modes : base + 2 * modes]
            if f == 0:
                parts += [low_end, high_end, nothing, nothing]
            else:
                parts += [low_end, nothing, high_end, nothing]
        set_face(
            WEST + f,
            got[0 : 2 * count].astype(bf16),
            jnp.concatenate(parts, axis=0).astype(bf16),
        )
    pltpu.make_async_copy(blocks, blocks, load_sem).wait()
    relay()

    slot = [slots[0, d] for d in range(4)]
    base_out = []
    base_in = []
    couple = 0.0
    for d in range(4):
        out = 0.0
        for s in range(4):
            out = out + mm(faces[s], blocks[slot[s], slot[d]])
        base_out.append(out[0:count] + out[count : 2 * count])
        high, low = split(
            out[2 * count : 2 * count + corner_rows]
            + out[2 * count + corner_rows : 2 * count + 2 * corner_rows]
        )
        couple = couple + mm_nt(
            jnp.concatenate([high, low], axis=0),
            faces[d, 2 * count : 2 * count + 2 * corner_rows, :],
        )
        lift[d, 0:corner_rows] = high
        lift[d, corner_rows : 2 * corner_rows] = high
        lift[d, 2 * corner_rows : 3 * corner_rows] = low
        lift[d, 3 * corner_rows :] = jnp.zeros((corner_rows, width), bf16)
        if d < 2:
            high = faces[d, 2 * count : 2 * count + corner_rows]
            lift[4 + d, 0:corner_rows] = high
            lift[4 + d, corner_rows : 2 * corner_rows] = high
            lift[4 + d, 2 * corner_rows : 3 * corner_rows] = faces[
                d, 2 * count + corner_rows : 2 * count + 2 * corner_rows
            ]
            lift[4 + d, 3 * corner_rows :] = jnp.zeros((corner_rows, width), bf16)
        base_in.append(
            faces[d, 0:count].astype(f32) + faces[d, count : 2 * count].astype(f32)
        )
    high, low = split(fold(couple))
    couple = jnp.concatenate([high, high, low, jnp.zeros_like(low)], axis=0)
    base_coarse = project([(base_out[d], d) for d in range(4)])
    base_inner = inner([(base_in[d], base_out[d]) for d in range(4)])
    start_inner = inner([(residual[f], scaled[f]) for f in range(2)])

    arrive("relay")
    lane_at = iota((lanes, 2 * lanes), 1)
    lane_mode = quotient(remainder(lane_at, lanes), count)
    base_lane = iota((lanes, 2 * lanes), 0) - lane_mode - jnp.where(lane_at < lanes, 0, half)
    row_at = iota((order, lanes), 0)
    base_row = jnp.where(row_at < half, row_at, row_at - half) - quotient(iota((order, lanes), 1), count)
    for v in range(4):
        first_at = place_in[v] * modes
        take = flags(base_lane == jnp.where(first_at >= half, first_at, -order * lanes))
        across = flags(base_row == jnp.where(first_at < half, first_at, -order * lanes))
        mine = halves(inverses[lax.rem(owner[v], 2), lax.div(owner[v], 2)])
        right = fold(mm(mine, take))
        left = lax.dot_general(mine, across, (((0,), (0,)), ((), ())), preferred_element_type=f32)
        coef[v * order : v * order + half, :] = left[0:half] + right[:, 0:lanes]
        coef[v * order + half : (v + 1) * order, :] = left[half:order] + right[:, lanes:]

    tile = flags(remainder(iota((2 * lanes, lanes), 0), count) == remainder(iota((2 * lanes, lanes), 1), count))
    mode_lane = quotient(iota((4 * order, lanes), 1), count) == remainder(iota((4 * order, lanes), 0), modes)

    def gathered(g):
        arrive(f"w{g}")
        parts = jnp.concatenate(split(wbuf[g].reshape(total_rows, lanes)), axis=1)
        picked = mm(pick[...], parts)
        picked = picked[:, 0:lanes] + picked[:, lanes:]
        chosen = jnp.where(mode_lane, picked[0 : 4 * order], 0.0)
        tiled = mm(jnp.concatenate(split(chosen), axis=1), tile) * coef[...]
        rows = [
            jnp.sum(tiled[v * order : (v + 1) * order], axis=0, keepdims=True) for v in range(4)
        ]
        return jnp.concatenate(rows, axis=1), picked[4 * order : 4 * order + 1]

    to_small = iota((wide_lanes, 4 * corner_rows), 1)
    shrink = flags(
        (quotient(iota((wide_lanes, 4 * corner_rows), 0), count) == remainder(to_small, corner_rows))
        & (to_small < 3 * corner_rows)
    )
    middle = quotient(iota((count, 4 * corner_rows), 1), corner_rows) == 1

    def shrunk(correction):
        small = fold(mm(halves(jnp.where(own_lane, correction, 0.0)), shrink))
        high, low = split(small)
        return small, jnp.where(middle, low.astype(f32), high.astype(f32)).astype(bf16)

    solved, _ = gathered(0)
    small, left = shrunk(solved)
    first_coarse = base_coarse + mm(left, couple)
    sums = pack(
        [
            start_inner + across_lanes(small, start_coarse),
            base_inner + across_lanes(small, base_coarse + first_coarse),
        ]
    )
    zmsg[1] = jnp.concatenate(
        [corner_rows_of(first_coarse), sums, jnp.zeros((3, lanes), f32)], axis=0
    )
    z_start(1)

    def to_owner(k, values):
        for f in range(2):
            high, low = split(values[f])
            back_out[k, f] = mm_nt(high, perm[f]) + mm_nt(low, perm[f])
            single(
                f"back{k}{f}",
                back_out.at[k, f],
                back_in.at[k, f],
                back_send.at[k, f],
                back_recv.at[k, f],
                (west, south)[f],
            )

    product = [base_out[d] + mm(left, lift[d]) for d in range(4)]
    to_owner(0, product[2:])
    direct = [scaled[f] + mm(left, lift[4 + f]) for f in range(2)]
    w_start(1)
    applied = []
    for f in range(2):
        arrive(f"back0{f}")
        applied.append((product[f] + back_in[0, f]) * live[f])
        flux_out[f] = halves(applied[f] * weight[f])
        single(f"flux{f}", flux_out.at[f], flux_in.at[f], flux_send.at[f], flux_recv.at[f], (east, north)[f])
    applied_coarse = project([(applied[f], f) for f in range(2)])
    applied_inner = inner([(scaled[f], applied[f]) for f in range(2)])
    applied_twice = inner([(applied[f] * weight[f], applied[f]) for f in range(2)])
    own_flux = [flux_out[f] for f in range(2)]
    for f in range(2):
        arrive(f"flux{f}")
        own_flux.append(mm(flux_in[f], perm[f]).astype(bf16))
    flux_product = []
    for d in range(4):
        out = 0.0
        for s in range(4):
            out = out + mm(own_flux[s], blocks[slot[s], slot[d]])
        flux_product.append(fold(out))

    flux_coarse = project([(flux_product[d], d) for d in range(4)])
    cross_inner = inner([(base_in[d], flux_product[d]) for d in range(4)])
    flux_inner = inner([(fold(own_flux[d].astype(f32)), flux_product[d]) for d in range(4)])

    change, sums = gathered(1)
    product_start = unpack(sums, 0)
    curvature = unpack(sums, 1)
    step = product_start / curvature
    step_row = as_row(step)
    solved = solved - jnp.concatenate([step_row] * 4, axis=1) * change
    small, left = shrunk(solved)
    moved = mm(left, couple)
    residual = [residual[f] - step * applied[f] for f in range(2)]
    weighted = [residual[f] * weight[f] for f in range(2)]
    zlast[...] = pack(
        [
            inner([(residual[f], weighted[f]) for f in range(2)])
            + across_lanes(small, start_coarse - step * applied_coarse),
            base_inner
            - step * (2.0 * cross_inner - step * flux_inner)
            + across_lanes(small, 2.0 * (base_coarse - step * flux_coarse) + moved),
            applied_inner - step * applied_twice + across_lanes(small, applied_coarse),
        ]
    )
    spread("zlast", zlast, zlast_buf, rank, z_send.at[2], z_recv.at[2], z_peer, team - 1)
    zlast_buf[rank] = zlast[...]
    fresh_product = [base_out[d] - step * flux_product[d] + mm(left, lift[d]) for d in range(4)]
    to_owner(1, fresh_product[2:])
    fresh = [weighted[f] + mm(left, lift[4 + f]) for f in range(2)]
    arrive("zlast")
    wlast[...] = jnp.sum(zlast_buf[...], axis=0)
    spread("wlast", wlast, wlast_buf, chip_at, w_send.at[2], w_recv.at[2], c_peer, chips - 1)
    wlast_buf[chip_at] = wlast[...]
    fresh_applied = []
    for f in range(2):
        arrive(f"back1{f}")
        fresh_applied.append((fresh_product[f] + back_in[1, f]) * live[f])
    arrive("wlast")
    sums = jnp.sum(wlast_buf[...], axis=0)
    product_fresh = unpack(sums, 0)
    ratio = product_fresh / product_start
    last_curvature = unpack(sums, 1) + 2.0 * ratio * unpack(sums, 2) + ratio * ratio * curvature
    last_step = product_fresh / last_curvature
    for f in range(2):
        sol_out[:, f, :] = step * direct[f] + last_step * (fresh[f] + ratio * direct[f])
        res_out[:, f, :] = residual[f] - last_step * (fresh_applied[f] + ratio * applied[f])

    for wait in list(pending.values()):
        wait()


def body(sources, schur, scaling, basis, inverse, sizes, match, slots, corners):
    wide_count = lax.axis_size("wide")
    narrow_count = lax.axis_size("narrow")
    count, width = sources.shape[2], sources.shape[4]
    modes = basis.shape[4]
    order = inverse.shape[1]
    lanes = modes * count
    verts = narrow_count + 1
    team = 2 * narrow_count
    chips = wide_count // 2
    msg_rows = -(-(3 * verts + 1) // 8) * 8
    vmem = pl.BlockSpec(memory_space=pltpu.VMEM)
    hbm = pl.BlockSpec(memory_space=pltpu.HBM)
    dma = pltpu.SemaphoreType.DMA
    out = jax.ShapeDtypeStruct((count, 2, width), f32)
    corner_rows = 4 * modes
    sol, res = pl.pallas_call(
        kernel,
        out_shape=(out, out),
        in_specs=[hbm] * 9,
        out_specs=(vmem, vmem),
        scratch_shapes=[
            pltpu.VMEM((count, 2, width), f32),
            pltpu.VMEM((2, width), f32),
            pltpu.VMEM((2, 2, modes, width), f32),
            pltpu.VMEM((order, order), f32),
            pltpu.VMEM((2, width), jnp.int32),
            pltpu.VMEM((verts, wide_count + 1), jnp.int32),
            pltpu.SMEM((1, 2), jnp.int32),
            pltpu.SMEM((1, 4), jnp.int32),
            pltpu.SMEM((verts, wide_count + 1), jnp.int32),
            pltpu.VMEM((4, 4, width, width), bf16),
            pltpu.VMEM((4, 2 * count + 2 * corner_rows, width), bf16),
            pltpu.VMEM((6, 4 * corner_rows, width), bf16),
            pltpu.VMEM((2, width, width), bf16),
            pltpu.VMEM((4 * order + 16, chips * msg_rows), bf16),
            pltpu.VMEM((4 * order, lanes), f32),
            pltpu.VMEM((order // 2, lanes), f32),
            pltpu.VMEM((2, chips, order // 2, lanes), f32),
            pltpu.VMEM((2, 8, lanes), f32),
            pltpu.VMEM((2, team, 8, lanes), f32),
            pltpu.VMEM((2, msg_rows, lanes), f32),
            pltpu.VMEM((2, chips, msg_rows, lanes), f32),
            pltpu.VMEM((1, lanes), f32),
            pltpu.VMEM((team, 1, lanes), f32),
            pltpu.VMEM((1, lanes), f32),
            pltpu.VMEM((chips, 1, lanes), f32),
            pltpu.VMEM((2, 4 * count, width), bf16),
            pltpu.VMEM((2, 4 * count, width), bf16),
            pltpu.VMEM((2, 2 * count, width), bf16),
            pltpu.VMEM((2, 2 * count, width), bf16),
            pltpu.VMEM((2, 2, count, width), f32),
            pltpu.VMEM((2, 2, count, width), f32),
            dma((9,)),
            dma,
            dma((3,)),
            dma((3,)),
            dma((3,)),
            dma((3,)),
            dma((2,)),
            dma((2,)),
            dma((2,)),
            dma((2,)),
            dma((2, 2)),
            dma((2, 2)),
            dma((2,)),
            dma((2,)),
        ],
        compiler_params=pltpu.CompilerParams(
            collective_id=0, has_side_effects=True, vmem_limit_bytes=48 << 20
        ),
    )(
        *(
            pltpu.with_memory_space_constraint(x, pltpu.HBM)
            for x in (
                sources[0, 0],
                schur[0, 0],
                scaling[0, 0],
                basis[0, 0],
                inverse[0],
                sizes[0],
                match[0, 0],
                slots[0],
                corners.T,
            )
        )
    )
    return sol[None, None], res[None, None]


def solution(mesh):
    placed = (
        P("wide", "narrow", None, None, None),
        P("wide", "narrow", None, None),
        P("wide", "narrow", None, None),
        P("wide", "narrow", None, None, None, None),
        P("wide", None, None),
        P("wide", "narrow", None),
        P("wide", "narrow", None, None),
        P("wide", "narrow", None),
        P(),
    )
    return jax.shard_map(
        body,
        mesh=mesh,
        in_specs=placed,
        out_specs=(P("wide", "narrow", None, None, None), P("wide", "narrow", None, None, None)),
        check_vma=False,
    )
```

```python
import jax
import jax.numpy as jnp
from jax import lax
from jax.experimental import pallas as pl
from jax.experimental.pallas import tpu as pltpu
from jax.sharding import PartitionSpec as P

MESH = pl.DeviceIdType.MESH
f32 = jnp.float32
bf16 = jnp.bfloat16
NT = (((1,), (1,)), ((), ()))
EAST, NORTH, WEST, SOUTH = range(4)


def iota(shape, dim):
    return lax.broadcasted_iota(jnp.int32, shape, dim)


def quotient(x, n):
    return x >> (n.bit_length() - 1) if n & (n - 1) == 0 else lax.div(x, jnp.int32(n))


def remainder(x, n):
    return x & (n - 1) if n & (n - 1) == 0 else lax.rem(x, jnp.int32(n))


def flags(x):
    return jnp.where(x, 1.0, 0.0).astype(bf16)


def mm(a, b):
    return jnp.dot(a, b, preferred_element_type=f32)


def mm_nt(a, b):
    return lax.dot_general(a, b, NT, preferred_element_type=f32)


def split(x):
    high = x.astype(bf16)
    return high, (x - high.astype(f32)).astype(bf16)


def halves(x):
    return jnp.concatenate(split(x), axis=0)


def fold(x):
    rows = x.shape[0] // 2
    return x[:rows] + x[rows:]


def kernel(
    src_hbm,
    schur,
    scaling_hbm,
    basis_hbm,
    inverse_hbm,
    sizes_hbm,
    match_hbm,
    slots_hbm,
    corners_hbm,
    out_ref,
    src,
    scaling,
    basis,
    inverse,
    match,
    table,
    sizes,
    slots,
    corners,
    blocks,
    faces,
    lift,
    perm,
    pick,
    coef,
    packed,
    inverses,
    zmsg,
    zbuf,
    wmsg,
    wbuf,
    zlast,
    zlast_buf,
    wlast,
    wlast_buf,
    fore_out,
    fore_in,
    flux_out,
    flux_in,
    back_out,
    back_in,
    in_sem,
    load_sem,
    z_send,
    z_recv,
    w_send,
    w_recv,
    fore_send,
    fore_recv,
    flux_send,
    flux_recv,
    back_send,
    back_recv,
    inv_send,
    inv_recv,
):
    wide_count = lax.axis_size("wide")
    narrow_count = lax.axis_size("narrow")
    wide_at = lax.axis_index("wide")
    narrow_at = lax.axis_index("narrow")
    count = src.shape[0]
    width = src.shape[2]
    order = inverse.shape[0]
    half = order // 2
    modes = basis.shape[2]
    capacity = order // modes
    lanes = modes * count
    corner_rows = 4 * modes
    msg_rows = wmsg.shape[1]
    verts = narrow_count + 1

    chips = wide_count // 2
    chip_at = wide_at // 2
    core_at = lax.rem(wide_at, 2)
    team = 2 * narrow_count
    rank = 2 * narrow_at + core_at

    side = 4
    ring = chips // side

    def around(size):
        return sorted(range(size), key=lambda t: -min(t, size - t))

    z_peers = [
        (2 * chip_at + (lax.rem(core_at + c, 2) if c else core_at), lax.rem(narrow_at + t, narrow_count))
        for t in around(narrow_count)
        for c in (1, 0)
        if t or c
    ]
    plane = [(a, b) for a in range(ring) for b in range(side) if a or b]
    plane.sort(key=lambda at: -min(at[0], ring - at[0]) - min(at[1], side - at[1]))
    c_peers = [
        (
            2 * (lax.rem(lax.div(chip_at, side) + a, ring) * side + lax.rem(chip_at + b, side)) + core_at,
            narrow_at,
        )
        for a, b in plane
    ]

    east = (lax.rem(wide_at + 1, wide_count), narrow_at)
    west = (lax.rem(wide_at + wide_count - 1, wide_count), narrow_at)
    north = (wide_at, lax.rem(narrow_at + 1, narrow_count))
    south = (wide_at, lax.rem(narrow_at + narrow_count - 1, narrow_count))
    twin = (2 * chip_at + 1 - core_at, narrow_at)

    barrier = pltpu.get_barrier_semaphore()

    for device in z_peers + c_peers + [east, west]:
        pl.semaphore_signal(barrier, 1, device_id=device, device_id_type=MESH)

    loads = [
        pltpu.make_async_copy(a, b, in_sem.at[i])
        for i, (a, b) in enumerate(
            [
                (sizes_hbm, sizes),
                (src_hbm, src),
                (basis_hbm, basis),
                (scaling_hbm, scaling),
                (inverse_hbm, inverse),
                (match_hbm, match),
                (slots_hbm, slots),
                (corners_hbm, corners),
                (corners_hbm, table),
            ]
        )
    ]
    for copy in loads:
        copy.start()

    for s in range(4):
        for t in range(4):
            pltpu.make_async_copy(
                schur.at[pl.ds(s * width, width), pl.ds(t * width, width)],
                blocks.at[s, t],
                load_sem,
            ).start()

    pending = {}

    def remote(a, b, send, recv, device):
        return pltpu.make_async_remote_copy(
            src_ref=a, dst_ref=b, send_sem=send, recv_sem=recv, device_id=device, device_id_type=MESH
        )

    def wait_bytes(ref, number, sem):
        part = ref.at[pl.ds(0, number)]
        pltpu.make_async_copy(part, part, sem).wait()

    def spread(name, a, buf, at, send, recv, peers, rows=None):
        to = buf.at[at]
        held = buf
        if rows is not None:
            a, to, held = a.at[pl.ds(0, rows)], to.at[pl.ds(0, rows)], buf.at[:, pl.ds(0, rows)]

        number = len(peers)
        for peer in peers:
            remote(a, to, send, recv, peer).start()
        pending["send " + name] = lambda: wait_bytes(held, number, send)
        pending[name] = lambda: wait_bytes(held, number, recv)

    def single(name, a, b, send, recv, device):
        copy = remote(a, b, send, recv, device)
        copy.start()
        pending["send " + name] = copy.wait_send
        pending[name] = copy.wait_recv

    def arrive(name):
        pending.pop(name)()

    for copy in loads[:4]:
        copy.wait()
    place = iota((1, width), 1)
    live = [(place < sizes[0, f]).astype(f32) for f in range(2)]
    weight = [scaling[f : f + 1, :] * live[f] for f in range(2)]
    residual = [src[:, f, :] * live[f] for f in range(2)]
    scaled = [residual[f] * weight[f] for f in range(2)]
    vec = [[basis[f, e] * live[f] for e in range(2)] for f in range(2)]
    nothing = jnp.zeros((modes, width), f32)

    for f in range(2):
        fore_out[f, 0 : 2 * count, :] = halves(scaled[f])
        fore_out[f, 2 * count : 4 * count, :] = halves(jnp.concatenate(vec[f], axis=0))

    def set_face(d, scaled_parts, ends):
        faces[d, 0 : 2 * count, :] = scaled_parts
        faces[d, 2 * count : 2 * count + 2 * corner_rows, :] = ends

    set_face(
        EAST,
        halves(scaled[0]),
        halves(jnp.concatenate([nothing, nothing, vec[0][0], vec[0][1]], axis=0)),
    )
    set_face(
        NORTH,
        halves(scaled[1]),
        halves(jnp.concatenate([nothing, vec[1][0], nothing, vec[1][1]], axis=0)),
    )

    wide_lanes = 4 * lanes
    grow = flags(remainder(iota((2 * corner_rows, wide_lanes), 0), corner_rows) == quotient(iota((2 * corner_rows, wide_lanes), 1), count))
    own_lane = remainder(iota((count, wide_lanes), 1), count) == iota((count, wide_lanes), 0)
    own_lane_one = own_lane[:, 0:lanes]

    def project(pairs):
        total = 0.0
        for values, d in pairs:
            total = total + mm_nt(
                halves(values), faces[d, 2 * count : 2 * count + 2 * corner_rows, :]
            )
        return fold(total)

    def corner_rows_of(projected):
        spread_out = fold(mm(halves(projected), grow))
        row = jnp.sum(jnp.where(own_lane, spread_out, 0.0), axis=0, keepdims=True)
        return jnp.concatenate([row[:, v * lanes : (v + 1) * lanes] for v in range(4)], axis=0)

    def across_lanes(a, b):
        return jnp.sum(a[:, 0 : 2 * corner_rows] * b, axis=1, keepdims=True)

    def inner(pairs):
        total = 0.0
        for a, b in pairs:
            total = total + jnp.sum(a * b, axis=1, keepdims=True)
        return total

    lane_one = iota((count, lanes), 1)
    row_one = iota((count, lanes), 0)

    def pack(values):
        out = jnp.zeros((count, lanes), f32)
        for g, value in enumerate(values):
            out = out + jnp.where(lane_one == g * count + row_one, value, 0.0)
        return jnp.sum(out, axis=0, keepdims=True)

    def unpack(row, g):
        return jnp.sum(jnp.where(lane_one == g * count + row_one, row, 0.0), axis=1, keepdims=True)

    def as_row(value):
        return jnp.sum(jnp.where(own_lane_one, value, 0.0), axis=0, keepdims=True)

    for g in range(2):
        zbuf[g, :, 4 + g : 8, :] = jnp.zeros((team, 4 - g, lanes), f32)
        wbuf[g, :, 3 * verts + g : msg_rows, :] = jnp.zeros(
            (chips, msg_rows - 3 * verts - g, lanes), f32
        )
    start_coarse = project([(residual[0], EAST), (residual[1], NORTH)])
    first = corner_rows_of(start_coarse)
    zmsg[0] = jnp.concatenate([first, jnp.zeros((4, lanes), f32)], axis=0)

    loads[4].wait()
    from_lane = iota((order, lanes), 0)
    to_lane = iota((order, lanes), 1)
    top = flags((from_lane == to_lane) & (to_lane < order))
    corner = flags((from_lane == to_lane - half) & (to_lane >= order))
    packed[...] = fold(mm(halves(inverse[0:half, :]), top)) + fold(
        mm(halves(inverse[half:order, :]), corner)
    )

    msg_at = iota((msg_rows, 8 * team), 0)
    from_at = iota((msg_rows, 8 * team), 1)
    from_row = from_at & 7
    from_col = (from_at >> 3) & 1
    from_sub = from_at >> 4
    goes = (from_col + (from_row >> 1)) * verts + from_sub + (from_row & 1)
    goes = jnp.where(from_row < 4, goes, jnp.where(from_row == 4, 3 * verts, -1))
    merge = flags(msg_at == goes)

    pl.semaphore_wait(barrier, len(z_peers) + len(c_peers) + 2)

    def z_start(g):
        spread(f"z{g}", zmsg.at[g], zbuf.at[g], rank, z_send.at[g], z_recv.at[g], z_peers, 4 + g)
        zbuf[g, rank] = zmsg[g]

    def w_start(g):
        arrive(f"z{g}")
        high, low = split(zbuf[g].reshape(8 * team, lanes))
        wmsg[g] = mm(merge, high) + mm(merge, low)
        spread(f"w{g}", wmsg.at[g], wbuf.at[g], chip_at, w_send.at[g], w_recv.at[g], c_peers, 3 * verts + g)
        wbuf[g, chip_at] = wmsg[g]

    z_start(0)
    for f in range(2):
        single(f"fore{f}", fore_out.at[f], fore_in.at[f], fore_send.at[f], fore_recv.at[f], (east, north)[f])
    spread("inv", packed, inverses.at[core_at], chip_at, inv_send.at[0], inv_recv.at[0], c_peers)
    inverses[core_at, chip_at] = packed[...]

    for copy in loads[5:]:
        copy.wait()
    for f in range(2):
        perm[f] = flags(iota((width, width), 0) == match[f : f + 1, :])
    vertex = [
        corners[narrow_at, wide_at],
        corners[narrow_at + 1, wide_at],
        corners[narrow_at, wide_at + 1],
        corners[narrow_at + 1, wide_at + 1],
    ]
    owner = [lax.div(v, capacity) for v in vertex]
    place_in = [v - b * capacity for v, b in zip(vertex, owner)]
    total_rows = chips * msg_rows
    in_msg = remainder(iota((1, total_rows), 1), msg_rows)
    in_col = (in_msg >= verts).astype(jnp.int32) + (in_msg >= 2 * verts).astype(jnp.int32)
    column = 2 * quotient(iota((1, total_rows), 1), msg_rows) + in_col
    column = jnp.where(in_msg < 3 * verts, column, -1)
    reach = flags(iota((wide_count + 1, total_rows), 0) == column)
    each = 0.0
    for part in split(table[...].astype(f32)):
        each = each + mm(part, reach)
    row_slots = jnp.sum(jnp.where(iota((verts, total_rows), 0) == in_msg - verts * in_col, each, 0.0), axis=0, keepdims=True)
    row_slots = jnp.where(in_msg < 3 * verts, row_slots, -1.0)
    for v in range(4):
        wanted = (owner[v] * capacity + quotient(iota((order, 1), 0), modes)).astype(f32)
        pick[v * order : (v + 1) * order, :] = flags(wanted == row_slots)
    pick[4 * order : 4 * order + 16, :] = flags(jnp.broadcast_to(in_msg, (16, total_rows)) == 3 * verts)

    w_start(0)

    def relay():
        arrive("inv")
        half_held = inverses.at[core_at]
        single("relay", half_held, half_held, inv_send.at[1], inv_recv.at[1], twin)


    for f in range(2):
        arrive(f"fore{f}")
        got = mm(fore_in[f], perm[f])
        parts = []
        for base in (2 * count, 2 * count + 2 * modes):
            low_end = got[base : base + modes]
            high_end = got[base + modes : base + 2 * modes]
            if f == 0:
                parts += [low_end, high_end, nothing, nothing]
            else:
                parts += [low_end, nothing, high_end, nothing]
        set_face(
            WEST + f,
            got[0 : 2 * count].astype(bf16),
            jnp.concatenate(parts, axis=0).astype(bf16),
        )
    pltpu.make_async_copy(blocks, blocks, load_sem).wait()
    relay()

    slot = [slots[0, d] for d in range(4)]
    base_out = []
    base_in = []
    couple = 0.0
    for d in range(4):
        out = 0.0
        for s in range(4):
            out = out + mm(faces[s], blocks[slot[s], slot[d]])
        base_out.append(out[0:count] + out[count : 2 * count])
        high, low = split(
            out[2 * count : 2 * count + corner_rows]
            + out[2 * count + corner_rows : 2 * count + 2 * corner_rows]
        )
        couple = couple + mm_nt(
            jnp.concatenate([high, low], axis=0),
            faces[d, 2 * count : 2 * count + 2 * corner_rows, :],
        )
        lift[d, 0:corner_rows] = high
        lift[d, corner_rows : 2 * corner_rows] = high
        lift[d, 2 * corner_rows : 3 * corner_rows] = low
        lift[d, 3 * corner_rows :] = jnp.zeros((corner_rows, width), bf16)
        if d < 2:
            high = faces[d, 2 * count : 2 * count + corner_rows]
            lift[4 + d, 0:corner_rows] = high
            lift[4 + d, corner_rows : 2 * corner_rows] = high
            lift[4 + d, 2 * corner_rows : 3 * corner_rows] = faces[
                d, 2 * count + corner_rows : 2 * count + 2 * corner_rows
            ]
            lift[4 + d, 3 * corner_rows :] = jnp.zeros((corner_rows, width), bf16)
        base_in.append(
            faces[d, 0:count].astype(f32) + faces[d, count : 2 * count].astype(f32)
        )
    high, low = split(fold(couple))
    couple = jnp.concatenate([high, high, low, jnp.zeros_like(low)], axis=0)
    base_coarse = project([(base_out[d], d) for d in range(4)])
    base_inner = inner([(base_in[d], base_out[d]) for d in range(4)])
    start_inner = inner([(residual[f], scaled[f]) for f in range(2)])

    arrive("relay")
    lane_at = iota((lanes, 2 * lanes), 1)
    lane_mode = quotient(remainder(lane_at, lanes), count)
    base_lane = iota((lanes, 2 * lanes), 0) - lane_mode - jnp.where(lane_at < lanes, 0, half)
    row_at = iota((order, lanes), 0)
    base_row = jnp.where(row_at < half, row_at, row_at - half) - quotient(iota((order, lanes), 1), count)
    for v in range(4):
        first_at = place_in[v] * modes
        take = flags(base_lane == jnp.where(first_at >= half, first_at, -order * lanes))
        across = flags(base_row == jnp.where(first_at < half, first_at, -order * lanes))
        mine = halves(inverses[lax.rem(owner[v], 2), lax.div(owner[v], 2)])
        right = fold(mm(mine, take))
        left = lax.dot_general(mine, across, (((0,), (0,)), ((), ())), preferred_element_type=f32)
        coef[v * order : v * order + half, :] = left[0:half] + right[:, 0:lanes]
        coef[v * order + half : (v + 1) * order, :] = left[half:order] + right[:, lanes:]

    tile = flags(remainder(iota((2 * lanes, lanes), 0), count) == remainder(iota((2 * lanes, lanes), 1), count))
    mode_lane = quotient(iota((4 * order, lanes), 1), count) == remainder(iota((4 * order, lanes), 0), modes)

    def gathered(g):
        arrive(f"w{g}")
        parts = jnp.concatenate(split(wbuf[g].reshape(total_rows, lanes)), axis=1)
        picked = mm(pick[...], parts)
        picked = picked[:, 0:lanes] + picked[:, lanes:]
        chosen = jnp.where(mode_lane, picked[0 : 4 * order], 0.0)
        tiled = mm(jnp.concatenate(split(chosen), axis=1), tile) * coef[...]
        rows = [
            jnp.sum(tiled[v * order : (v + 1) * order], axis=0, keepdims=True) for v in range(4)
        ]
        return jnp.concatenate(rows, axis=1), picked[4 * order : 4 * order + 1]

    to_small = iota((wide_lanes, 4 * corner_rows), 1)
    shrink = flags(
        (quotient(iota((wide_lanes, 4 * corner_rows), 0), count) == remainder(to_small, corner_rows))
        & (to_small < 3 * corner_rows)
    )
    middle = quotient(iota((count, 4 * corner_rows), 1), corner_rows) == 1

    def shrunk(correction):
        small = fold(mm(halves(jnp.where(own_lane, correction, 0.0)), shrink))
        high, low = split(small)
        return small, jnp.where(middle, low.astype(f32), high.astype(f32)).astype(bf16)

    solved, _ = gathered(0)
    small, left = shrunk(solved)
    first_coarse = base_coarse + mm(left, couple)
    sums = pack(
        [
            start_inner + across_lanes(small, start_coarse),
            base_inner + across_lanes(small, base_coarse + first_coarse),
        ]
    )
    zmsg[1] = jnp.concatenate(
        [corner_rows_of(first_coarse), sums, jnp.zeros((3, lanes), f32)], axis=0
    )
    z_start(1)

    def to_owner(k, values):
        for f in range(2):
            high, low = split(values[f])
            back_out[k, f] = mm_nt(high, perm[f]) + mm_nt(low, perm[f])
            single(
                f"back{k}{f}",
                back_out.at[k, f],
                back_in.at[k, f],
                back_send.at[k, f],
                back_recv.at[k, f],
                (west, south)[f],
            )

    product = [base_out[d] + mm(left, lift[d]) for d in range(4)]
    to_owner(0, product[2:])
    direct = [scaled[f] + mm(left, lift[4 + f]) for f in range(2)]
    w_start(1)
    applied = []
    for f in range(2):
        arrive(f"back0{f}")
        applied.append((product[f] + back_in[0, f]) * live[f])
        flux_out[f] = halves(applied[f] * weight[f])
        single(f"flux{f}", flux_out.at[f], flux_in.at[f], flux_send.at[f], flux_recv.at[f], (east, north)[f])
    applied_coarse = project([(applied[f], f) for f in range(2)])
    applied_inner = inner([(scaled[f], applied[f]) for f in range(2)])
    applied_twice = inner([(applied[f] * weight[f], applied[f]) for f in range(2)])
    own_flux = [flux_out[f] for f in range(2)]
    for f in range(2):
        arrive(f"flux{f}")
        own_flux.append(mm(flux_in[f], perm[f]).astype(bf16))
    flux_product = []
    for d in range(4):
        out = 0.0
        for s in range(4):
            out = out + mm(own_flux[s], blocks[slot[s], slot[d]])
        flux_product.append(fold(out))

    flux_coarse = project([(flux_product[d], d) for d in range(4)])
    cross_inner = inner([(base_in[d], flux_product[d]) for d in range(4)])
    flux_inner = inner([(fold(own_flux[d].astype(f32)), flux_product[d]) for d in range(4)])

    change, sums = gathered(1)
    product_start = unpack(sums, 0)
    curvature = unpack(sums, 1)
    step = product_start / curvature
    step_row = as_row(step)
    solved = solved - jnp.concatenate([step_row] * 4, axis=1) * change
    small, left = shrunk(solved)
    moved = mm(left, couple)
    residual = [residual[f] - step * applied[f] for f in range(2)]
    weighted = [residual[f] * weight[f] for f in range(2)]
    zlast[...] = pack(
        [
            inner([(residual[f], weighted[f]) for f in range(2)])
            + across_lanes(small, start_coarse - step * applied_coarse),
            base_inner
            - step * (2.0 * cross_inner - step * flux_inner)
            + across_lanes(small, 2.0 * (base_coarse - step * flux_coarse) + moved),
            applied_inner - step * applied_twice + across_lanes(small, applied_coarse),
        ]
    )
    spread("zlast", zlast, zlast_buf, rank, z_send.at[2], z_recv.at[2], z_peers)
    zlast_buf[rank] = zlast[...]
    fresh_product = [base_out[d] - step * flux_product[d] + mm(left, lift[d]) for d in range(4)]
    to_owner(1, fresh_product[2:])
    fresh = [weighted[f] + mm(left, lift[4 + f]) for f in range(2)]
    arrive("zlast")
    wlast[...] = jnp.sum(zlast_buf[...], axis=0)
    spread("wlast", wlast, wlast_buf, chip_at, w_send.at[2], w_recv.at[2], c_peers)
    wlast_buf[chip_at] = wlast[...]
    fresh_applied = []
    for f in range(2):
        arrive(f"back1{f}")
        fresh_applied.append((fresh_product[f] + back_in[1, f]) * live[f])
    arrive("wlast")
    sums = jnp.sum(wlast_buf[...], axis=0)
    product_fresh = unpack(sums, 0)
    ratio = product_fresh / product_start
    last_curvature = unpack(sums, 1) + 2.0 * ratio * unpack(sums, 2) + ratio * ratio * curvature
    last_step = product_fresh / last_curvature
    for f in range(2):
        out_ref[0, :, f, :] = step * direct[f] + last_step * (fresh[f] + ratio * direct[f])
        out_ref[1, :, f, :] = residual[f] - last_step * (fresh_applied[f] + ratio * applied[f])

    for wait in list(pending.values()):
        wait()


def body(sources, schur, scaling, basis, inverse, sizes, match, slots, corners):
    wide_count = lax.axis_size("wide")
    narrow_count = lax.axis_size("narrow")
    count, width = sources.shape[2], sources.shape[4]
    modes = basis.shape[4]
    order = inverse.shape[1]
    lanes = modes * count
    verts = narrow_count + 1
    team = 2 * narrow_count
    chips = wide_count // 2
    msg_rows = -(-(3 * verts + 1) // 8) * 8
    vmem = pl.BlockSpec(memory_space=pltpu.VMEM)
    hbm = pl.BlockSpec(memory_space=pltpu.HBM)
    dma = pltpu.SemaphoreType.DMA
    out = jax.ShapeDtypeStruct((2, count, 2, width), f32)
    corner_rows = 4 * modes
    both = pl.pallas_call(
        kernel,
        out_shape=out,
        in_specs=[hbm] * 9,
        out_specs=vmem,
        scratch_shapes=[
            pltpu.VMEM((count, 2, width), f32),
            pltpu.VMEM((2, width), f32),
            pltpu.VMEM((2, 2, modes, width), f32),
            pltpu.VMEM((order, order), f32),
            pltpu.VMEM((2, width), jnp.int32),
            pltpu.VMEM((verts, wide_count + 1), jnp.int32),
            pltpu.SMEM((1, 2), jnp.int32),
            pltpu.SMEM((1, 4), jnp.int32),
            pltpu.SMEM((verts, wide_count + 1), jnp.int32),
            pltpu.VMEM((4, 4, width, width), bf16),
            pltpu.VMEM((4, 2 * count + 2 * corner_rows, width), bf16),
            pltpu.VMEM((6, 4 * corner_rows, width), bf16),
            pltpu.VMEM((2, width, width), bf16),
            pltpu.VMEM((4 * order + 16, chips * msg_rows), bf16),
            pltpu.VMEM((4 * order, lanes), f32),
            pltpu.VMEM((order // 2, lanes), f32),
            pltpu.VMEM((2, chips, order // 2, lanes), f32),
            pltpu.VMEM((2, 8, lanes), f32),
            pltpu.VMEM((2, team, 8, lanes), f32),
            pltpu.VMEM((2, msg_rows, lanes), f32),
            pltpu.VMEM((2, chips, msg_rows, lanes), f32),
            pltpu.VMEM((1, lanes), f32),
            pltpu.VMEM((team, 1, lanes), f32),
            pltpu.VMEM((1, lanes), f32),
            pltpu.VMEM((chips, 1, lanes), f32),
            pltpu.VMEM((2, 4 * count, width), bf16),
            pltpu.VMEM((2, 4 * count, width), bf16),
            pltpu.VMEM((2, 2 * count, width), bf16),
            pltpu.VMEM((2, 2 * count, width), bf16),
            pltpu.VMEM((2, 2, count, width), f32),
            pltpu.VMEM((2, 2, count, width), f32),
            dma((9,)),
            dma,
            dma((3,)),
            dma((3,)),
            dma((3,)),
            dma((3,)),
            dma((2,)),
            dma((2,)),
            dma((2,)),
            dma((2,)),
            dma((2, 2)),
            dma((2, 2)),
            dma((2,)),
            dma((2,)),
        ],
        compiler_params=pltpu.CompilerParams(
            collective_id=0, has_side_effects=True, vmem_limit_bytes=48 << 20
        ),
    )(
        *(
            pltpu.with_memory_space_constraint(x, pltpu.HBM)
            for x in (
                sources[0, 0],
                schur[0, 0],
                scaling[0, 0],
                basis[0, 0],
                inverse[0],
                sizes[0],
                match[0, 0],
                slots[0],
                corners.T,
            )
        )
    )
    return both[0][None, None], both[1][None, None]


def solution(mesh):
    placed = (
        P("wide", "narrow", None, None, None),
        P("wide", "narrow", None, None),
        P("wide", "narrow", None, None),
        P("wide", "narrow", None, None, None, None),
        P("wide", None, None),
        P("wide", "narrow", None),
        P("wide", "narrow", None, None),
        P("wide", "narrow", None),
        P(),
    )
    return jax.shard_map(
        body,
        mesh=mesh,
        in_specs=placed,
        out_specs=(P("wide", "narrow", None, None, None), P("wide", "narrow", None, None, None)),
        check_vma=False,
    )
```
